256 devices in a mesh: stream: 8 (over z_lo, core), azim: 32 (over z_hi, x, y).
Axes of the slice: x: 4, y: 4, z: 8 (z_hi: 2, z_lo: 4; z = z_hi * 4 + z_lo), core: 2. Of those that a mesh axis runs over, the one named last changes fastest.
Arguments:
- surface_signal: bfloat16 [64, 524288], P(None, ('stream', 'azim')), may hold values from -6 to 6
- retarded_weights: bfloat16 [4096, 64, 64], P(('stream', 'azim')), may hold values from -0.75 to 0.75
- radiation_weights: bfloat16 [1024, 524288], P(None, ('stream', 'azim')), may hold values from -0.03125 to 0.03125
- target_signal: float32 [64, 1024], replicated, may hold values from -6 to 6
- observer_weights: float32 [1024], replicated, may hold values from 0.5 to 2
- sample_weights: float32 [64], replicated, may hold values from 1 to 8
- host_element: int32 [524288], P(('stream', 'azim')), may hold values from 0 to 4095
- source_profile: float32 [320], replicated, may hold values from -6 to 6
- adjoint_state: bfloat16 [320, 32, 128, 256], P(None, 'stream', 'azim'), may hold values from -6 to 6
- volume_operator: bfloat16 [320, 320], replicated, may hold values from -0.3125 to 0.3125
- lift_operator: bfloat16 [320, 480], replicated, may hold values from -0.25 to 0.25
Outputs:
- obs_sens: float32 [64, 1024], P(None, 'azim')
- adjoint_next: float32 [320, 32, 128, 256], P(None, 'stream', 'azim')
The draws below stay inside these ranges and needn't reach their ends.
Inputs may be any that keep to these rules, and one draw needn't show every extreme that they name: host_element[i] numbers an element among the 4 x 4 x 256 elements of the device block that holds surface point i, as (x 4 + a) * 256 + r in that block.
All inputs are finite; a program needn't handle non-finite values.
Results may differ from the reference program's by a relative error of at most 0.0039.
Values may be sent and summed in bfloat16 or wider, within the bound.
A program may use at most 64 MiB of HBM per device.

```python
import math
import jax
import jax.numpy as jnp
from jax import lax

OBS = 1024
TW = 64
NVAR = 5
NODE = 4
BLK = 128
SURF_DEV = 2048
EXD = 4
EAD = 4
ER = 256
COMP = 320
FACE = 80
SURF = 524288
NBLK = 4096
NX = 32
NA = 128
N_AZIM = 32


def set_ends(entries, rng, least, top_value):
    index_at = [jax.random.randint(jax.random.fold_in(rng, axis), (), 0, length) for axis, length in enumerate(entries.shape)]
    widest = entries.shape.index(max(entries.shape))
    next_to = index_at[:widest] + [(index_at[widest] + 1) % entries.shape[widest]] + index_at[widest + 1:]
    return entries.at[tuple(index_at)].set(least).at[tuple(next_to)].set(top_value)


def spiked(values, key, source, target, blocks, factor):
    def block_of(dim):
        return (jnp.arange(values.shape[dim]) // (values.shape[dim] // blocks)).reshape((-1,) + (1,) * (values.ndim - 1 - dim))

    one_side = jax.random.permutation(key, blocks)[block_of(target)]
    second = (block_of(target) + blocks // 2) % blocks
    return jnp.where((block_of(source) == one_side) | (block_of(source) == second), factor * values, values)


def level_of(rng, shape, shards, smallest, top_value):
    loudness = 1.0
    for axis_at, blocks in shards:
        heights = jax.random.uniform(jax.random.fold_in(jax.random.fold_in(rng, 6), axis_at), (blocks,), jnp.float32, smallest / len(shards), top_value / len(shards))
        loudness = loudness * jnp.repeat(jnp.exp(heights), shape[axis_at] // blocks).reshape((-1,) + (1,) * (len(shape) - 1 - axis_at))
    return loudness


def gaussian(own_key, shape, scale, bound, cuts=(), kind=jnp.bfloat16):
    result = jax.random.normal(own_key, shape, jnp.float32) * scale
    if len(cuts) > 0:
        result = level_of(own_key, shape, cuts, -0.22, 0.18) * result
    return jnp.clip(result, min=-bound, max=bound).astype(kind)


def bell_draw_with(own_key, dims, scale, most, cuts, heavy, kind=jnp.bfloat16):
    entries = scale * jax.random.normal(own_key, dims, jnp.float32)
    if cuts:
        entries = entries * level_of(own_key, dims, cuts, -0.22, 0.18)
    return jnp.clip(spiked(entries, jax.random.fold_in(own_key, 3), *heavy), -most, most).astype(kind)


def setup_inputs(seed: int = 0) -> dict:
    keys = jax.random.split(jax.random.key(seed), 12)
    return {
        "surface_signal": gaussian(keys[0], (TW, SURF), 1.0, 6.0, ((1, 256),)),
        "retarded_weights": gaussian(keys[1], (NBLK, TW, TW), TW ** -0.5, 0.75, ((0, 256),)),
        "radiation_weights": bell_draw_with(keys[2], (OBS, SURF), SURF ** -0.5, 0.03125, ((1, 256),), (1, 0, 256, 6.0)),
        "target_signal": gaussian(keys[3], (TW, OBS), 1.0, 6.0, (), jnp.float32),
        "observer_weights": jnp.clip(jnp.exp(jax.random.uniform(keys[4], (OBS,), jnp.float32, math.log(0.5), math.log(2.0))), 0.5, 2.0),
        "sample_weights": jnp.clip(jnp.exp(jax.random.uniform(keys[5], (TW,), jnp.float32, math.log(1.0), math.log(8.0))), 1.0, 8.0),
        "host_element": set_ends(jax.random.randint(keys[6], (SURF,), 0, EXD * EAD * ER), jax.random.fold_in(keys[6], 1), 0, (EXD * EAD * ER) - 1).astype(jnp.int32),
        "source_profile": gaussian(keys[7], (COMP,), 1.0, 6.0, (), jnp.float32),
        "adjoint_state": gaussian(keys[8], (COMP, NX, NA, ER), 1.0, 6.0, ((1, 8), (2, 32))),
        "volume_operator": gaussian(keys[9], (COMP, COMP), COMP ** -0.5, 0.3125),
        "lift_operator": gaussian(keys[10], (COMP, 6 * FACE), (6 * FACE) ** -0.5, 0.25),
    }


def hann_taper(count):
    samples = jnp.arange(count, dtype=jnp.float32)
    return 0.5 - 0.5 * jnp.cos(2.0 * jnp.pi * (samples + 0.5) / count)


def plane_traces(plane):
    rest = plane.shape[1:]
    shaped = plane.reshape((NVAR, NODE, NODE, NODE) + rest)
    lower_axial = shaped[:, 0].reshape((FACE,) + rest)
    upper_axial = shaped[:, NODE - 1].reshape((FACE,) + rest)
    lower_sector = shaped[:, :, 0].reshape((FACE,) + rest)
    upper_sector = shaped[:, :, NODE - 1].reshape((FACE,) + rest)
    lower_radial = shaped[:, :, :, 0].reshape((FACE,) + rest)
    upper_radial = shaped[:, :, :, NODE - 1].reshape((FACE,) + rest)
    return lower_axial, upper_axial, lower_sector, upper_sector, lower_radial, upper_radial


def reference(surface_signal, retarded_weights, radiation_weights, target_signal, observer_weights, sample_weights, host_element, source_profile, adjoint_state, volume_operator, lift_operator):
    tapering = hann_taper(TW)
    blocked = surface_signal.reshape(TW, NBLK, BLK).astype(jnp.float32)
    delayed = jnp.einsum('bkt,kbs->tbs', retarded_weights.astype(jnp.float32), blocked)
    delayed_low = delayed.astype(jnp.bfloat16).reshape(TW, SURF)
    observer_signal = jnp.dot(delayed_low, radiation_weights.T, preferred_element_type=jnp.float32)
    obs_sens = observer_weights[None, :] * tapering[:, None] * (observer_signal - target_signal)
    sens_low = obs_sens.astype(jnp.bfloat16)
    spread = jnp.dot(sens_low, radiation_weights, preferred_element_type=jnp.float32)
    spread_low = spread.astype(jnp.bfloat16).reshape(TW, NBLK, BLK).astype(jnp.float32)
    source_time = jnp.einsum('bkt,tbs->kbs', retarded_weights.astype(jnp.float32), spread_low)
    strength = jnp.sum(source_time * sample_weights[:, None, None], axis=0).reshape(SURF)

    point_ids = jnp.arange(SURF, dtype=jnp.int32)
    device_ids = point_ids // SURF_DEV
    slab_ids = device_ids // N_AZIM
    sector_ids = device_ids % N_AZIM
    local_axial = host_element // (EAD * ER)
    local_sector = (host_element // ER) % EAD
    local_radial = host_element % ER
    flat_ids = ((slab_ids * EXD + local_axial) * NA + sector_ids * EAD + local_sector) * ER + local_radial
    element_source = jax.ops.segment_sum(strength, flat_ids.astype(jnp.int32), num_segments=NX * NA * ER)
    source_grid = element_source.reshape(NX, NA, ER)

    def plane_update(plane_index):
        current = lax.dynamic_index_in_dim(adjoint_state, plane_index, 1, keepdims=False)
        previous = lax.dynamic_index_in_dim(adjoint_state, jnp.maximum(plane_index - 1, 0), 1, keepdims=False)
        following = lax.dynamic_index_in_dim(adjoint_state, jnp.minimum(plane_index + 1, NX - 1), 1, keepdims=False)
        own_traces = plane_traces(current)
        from_lower_axial = jnp.where(plane_index > 0, plane_traces(previous)[1], jnp.zeros_like(own_traces[1]))
        from_upper_axial = jnp.where(plane_index < NX - 1, plane_traces(following)[0], jnp.zeros_like(own_traces[0]))
        from_lower_sector = jnp.roll(own_traces[3], 1, axis=1)
        from_upper_sector = jnp.roll(own_traces[2], -1, axis=1)
        zero_rim = jnp.zeros_like(own_traces[5][..., :1])
        from_lower_radial = jnp.concatenate([zero_rim, own_traces[5][..., :-1]], axis=2)
        from_upper_radial = jnp.concatenate([own_traces[4][..., 1:], zero_rim], axis=2)
        stacked = jnp.concatenate([from_lower_axial, from_upper_axial, from_lower_sector, from_upper_sector, from_lower_radial, from_upper_radial], axis=0).reshape(6 * FACE, NA * ER)
        flat_current = current.reshape(COMP, NA * ER)
        volume_term = jnp.dot(volume_operator, flat_current, preferred_element_type=jnp.float32)
        face_term = jnp.dot(lift_operator, stacked, preferred_element_type=jnp.float32)
        plane_source = lax.dynamic_index_in_dim(source_grid, plane_index, 0, keepdims=False).reshape(1, NA * ER)
        updated = flat_current.astype(jnp.float32) + volume_term + face_term + source_profile[:, None] * plane_source
        return updated.reshape(COMP, NA, ER)

    planes = lax.map(plane_update, jnp.arange(NX, dtype=jnp.int32))
    adjoint_next = jnp.transpose(planes, (1, 0, 2, 3))
    return obs_sens, adjoint_next
```

```python
import jax
import jax.numpy as jnp
import numpy as np
from jax import lax
from jax.experimental import pallas as pl
from jax.experimental.pallas import tpu as pltpu
from jax.sharding import PartitionSpec as P

MESH = pl.DeviceIdType.MESH
BF = jnp.bfloat16
F32 = jnp.float32
ANY = pl.BlockSpec(memory_space=pl.ANY)
VM = pl.BlockSpec(memory_space=pltpu.VMEM)
ROWS = 32
NT = (((1,), (1,)), ((), ()))
TN = (((0,), (0,)), ((), ()))


def dot(a, b, dims=(((1,), (0,)), ((), ()))):
    return lax.dot_general(a, b, dims, preferred_element_type=F32)


def halves(x):
    top = x.astype(BF)
    return top, (x - top.astype(F32)).astype(BF)


def peers_by_distance():
    def hops(d):
        return min(d, 4 - d)

    steps = [(dx, dy, dc) for dx in range(4) for dy in range(4) for dc in range(2)]
    steps = [s for s in steps if s != (0, 0, 0)]
    return sorted(steps, key=lambda s: -(hops(s[0]) + hops(s[1])))


def expander():
    e = np.zeros((480, 640), np.float32)
    for j in range(160):
        e[j, j] = 1.0
    for vp in range(20):
        for w in range(4):
            e[160 + vp * 4 + w, 160 + vp * 8 + 4 + w] = 1.0
            e[240 + vp * 4 + w, 320 + vp * 8 + w] = 1.0
    for j in range(160):
        e[320 + j, 480 + j] = 1.0
    return e


def kernel(
    sig_hbm, ret_hbm, rad_hbm, state_hbm, lift_hbm, vol_hbm, exp_hbm, target_hbm,
    taper_ref, wobs_ref, wsam_ref, host_ref,
    base_hbm, obs_ref, es_ref,
    sig, ret, rad, st, lift, vol, exp, target,
    d0, d1, g0, g1, part, recv_a, send_b, recv_b, sens, own_f, other_f,
    sf, rhs, lf, az_send, az_recv, oh_lo, tcol,
    ld, out_sem, sa, ra, sb, rb, sc, rc, sp, rp, hx_s, hx_r, ha_s, ha_r,
):
    s = lax.axis_index("stream")
    a = lax.axis_index("azim")
    core = s % 2
    z_lo = s // 2
    xy = a % 16
    z_hi = a // 16
    cx, cy = xy // 4, xy % 4
    q_me = core * 16 + xy
    z_me = z_hi * 4 + z_lo
    steps = peers_by_distance()

    def group_peer(step):
        dx, dy, dc = step
        return z_lo * 2 + (core + dc) % 2, z_hi * 16 + ((cx + dx) % 4) * 4 + (cy + dy) % 4

    def z_peer(dz):
        z = (z_me + dz) % 8
        return (z % 4) * 2 + core, (z // 4) * 16 + xy

    def q_of(peer):
        return (peer[0] % 2) * 16 + peer[1] % 16

    a_next, a_prev = (a + 1) % 32, (a + 31) % 32

    loads = {}

    def load(i, src, dst):
        loads[i] = pltpu.make_async_copy(src, dst, ld.at[i])
        loads[i].start()

    load(0, ret_hbm, ret)
    load(1, sig_hbm, sig)
    for c in range(4):
        load(2 + c, rad_hbm.at[pl.ds(c * 8, 8)], rad.at[pl.ds(c * 8, 8)])
    load(6, state_hbm, st)
    load(7, lift_hbm, lift)
    load(8, exp_hbm, exp)
    load(9, vol_hbm, vol)
    load(10, target_hbm, target)

    barrier = pltpu.get_barrier_semaphore()

    def greet(peer):
        pl.semaphore_signal(barrier, inc=1, device_id=peer, device_id_type=MESH)

    for step in steps:
        greet(group_peer(step))
    for dz in range(1, 8):
        greet(z_peer(dz))
    greet((s, a_next))
    greet((s, a_prev))

    @pl.when(s > 0)
    def _():
        greet((s - 1, a))

    @pl.when(s < 7)
    def _():
        greet((s + 1, a))

    loads[0].wait()
    loads[1].wait()
    d0[64:128, :] = jnp.zeros((64, 2048), BF)
    d1[0:64, :] = jnp.zeros((64, 2048), BF)
    for b in range(16):
        cols = slice(b * 128, b * 128 + 128)
        blk = dot(ret[b], sig[:, cols], TN).astype(BF)
        d0[0:64, cols] = blk
        d1[64:128, cols] = blk
    for c in range(4):
        loads[2 + c].wait()
    for g in range(2):
        q0 = g * 16
        acc = dot(rad[q0 : q0 + 16, 0].reshape(256, 2048), d0[...], NT)
        acc = acc + dot(rad[q0 : q0 + 16, 1].reshape(256, 2048), d1[...], NT)
        part[q0 : q0 + 16] = acc.reshape(16, 16, 128).astype(BF)

    extra = jnp.where(s > 0, 1, 0) + jnp.where(s < 7, 1, 0)
    pl.semaphore_wait(barrier, 40 + extra)

    for step in steps:
        peer = group_peer(step)
        pltpu.make_async_remote_copy(
            src_ref=part.at[q_of(peer)], dst_ref=recv_a.at[q_me], send_sem=sa, recv_sem=ra,
            device_id=peer, device_id_type=MESH,
        ).start()
    recv_a[q_me] = part[q_me]

    loads[6].wait()

    @pl.loop(0, 10)
    def _(i):
        sf[pl.ds(i * 1024, 1024), :] = st[pl.ds(i * 32, 32)].astype(F32).reshape(1024, 128)

    lane = lax.broadcasted_iota(jnp.int32, (80, 128), 1)

    @pl.loop(0, 4)
    def _(x):
        for ay in range(4):
            roll_up, roll_dn = [], []
            for rhi in range(2):
                r = x * 8 + rhi * 4 + ay
                col = pl.multiple_of((x * 8 + ay * 2 + rhi) * 128, 128)
                f = sf[pl.ds(r, 320, stride=ROWS), :]
                xb = f.astype(BF)
                rhs[640:960, pl.ds(col, 128)] = xb
                x5 = xb.reshape(5, 64, 128)

                @pl.when(x < 3)
                def _():
                    rhs[0:80, pl.ds(col + 1024, 128)] = x5[:, 48:64].reshape(80, 128)

                @pl.when(x > 0)
                def _():
                    rhs[80:160, pl.ds(col - 1024, 128)] = x5[:, 0:16].reshape(80, 128)

                tiles = f.reshape(20, 2, 8, 128)
                upper = tiles[:, 1]
                lower = tiles[:, 0]
                if ay < 3:
                    rhs[160:320, pl.ds(col + 256, 128)] = upper.reshape(160, 128).astype(BF)
                else:
                    u = upper.reshape(10, 2, 8, 128)
                    packed = jnp.concatenate([u[:, 0, 4:8], u[:, 1, 4:8]], axis=1)
                    az_send[0, :, pl.ds(pl.multiple_of(x * 256 + rhi * 128, 128), 128)] = packed.reshape(80, 128).astype(BF)
                if ay > 0:
                    rhs[320:480, pl.ds(col - 256, 128)] = lower.reshape(160, 128).astype(BF)
                else:
                    u = lower.reshape(10, 2, 8, 128)
                    packed = jnp.concatenate([u[:, 0, 0:4], u[:, 1, 0:4]], axis=1)
                    az_send[1, :, pl.ds(pl.multiple_of(x * 256 + rhi * 128, 128), 128)] = packed.reshape(80, 128).astype(BF)
                roll_up.append(pltpu.roll(sf[pl.ds(3 * ROWS + r, 80, stride=4 * ROWS), :], 1, 1))
                roll_dn.append(pltpu.roll(sf[pl.ds(r, 80, stride=4 * ROWS), :], 127, 1))
            col = pl.multiple_of((x * 8 + ay * 2) * 128, 128)
            zero = jnp.zeros((80, 128), F32)
            rhs[480:560, pl.ds(col, 128)] = jnp.where(lane == 0, zero, roll_up[0]).astype(BF)
            rhs[480:560, pl.ds(col + 128, 128)] = jnp.where(lane == 0, roll_up[0], roll_up[1]).astype(BF)
            rhs[560:640, pl.ds(col, 128)] = jnp.where(lane == 127, roll_dn[1], roll_dn[0]).astype(BF)
            rhs[560:640, pl.ds(col + 128, 128)] = jnp.where(lane == 127, zero, roll_dn[1]).astype(BF)

    az_up = pltpu.make_async_remote_copy(
        src_ref=az_send.at[0], dst_ref=az_recv.at[0], send_sem=ha_s.at[0], recv_sem=ha_r.at[0],
        device_id=(s, a_next), device_id_type=MESH)
    az_dn = pltpu.make_async_remote_copy(
        src_ref=az_send.at[1], dst_ref=az_recv.at[1], send_sem=ha_s.at[1], recv_sem=ha_r.at[1],
        device_id=(s, a_prev), device_id_type=MESH)
    az_up.start()
    az_dn.start()

    @pl.when(s < 7)
    def _():
        for v in range(5):
            pltpu.make_async_remote_copy(
                src_ref=rhs.at[pl.ds(640 + v * 64 + 48, 16), pl.ds(3072, 1024)],
                dst_ref=rhs.at[pl.ds(v * 16, 16), pl.ds(0, 1024)],
                send_sem=hx_s.at[0], recv_sem=hx_r.at[0],
                device_id=(s + 1, a), device_id_type=MESH).start()

    @pl.when(s > 0)
    def _():
        for v in range(5):
            pltpu.make_async_remote_copy(
                src_ref=rhs.at[pl.ds(640 + v * 64, 16), pl.ds(0, 1024)],
                dst_ref=rhs.at[pl.ds(80 + v * 16, 16), pl.ds(3072, 1024)],
                send_sem=hx_s.at[1], recv_sem=hx_r.at[1],
                device_id=(s - 1, a), device_id_type=MESH).start()

    @pl.when(s == 0)
    def _():
        rhs[0:80, 0:1024] = jnp.zeros((80, 1024), BF)

    @pl.when(s == 7)
    def _():
        rhs[80:160, 3072:4096] = jnp.zeros((80, 1024), BF)

    loads[10].wait()
    kb = pl.multiple_of((q_me // 4) * 128, 128)
    row = pl.multiple_of((q_me % 4) * 32, 32)

    def packed_columns(block):
        tcol[...] = jnp.transpose(block)
        return jnp.concatenate(
            [tcol[pl.ds(row, 16), :], tcol[pl.ds(pl.multiple_of(row + 16, 16), 16), :]], axis=1)

    target_own = packed_columns(target[:, pl.ds(kb, 128)])
    weight_own = packed_columns(taper_ref[...] * wobs_ref[:, pl.ds(kb, 128)])

    pltpu.make_async_copy(part.at[pl.ds(0, 31)], recv_a.at[pl.ds(0, 31)], ra).wait()
    send_b[...] = jnp.sum(recv_a[...].astype(F32), axis=0).astype(BF)
    for dz in (4, 3, 5, 2, 6, 1, 7):
        pltpu.make_async_remote_copy(
            src_ref=send_b, dst_ref=recv_b.at[z_me], send_sem=sb, recv_sem=rb,
            device_id=z_peer(dz), device_id_type=MESH,
        ).start()
    recv_b[z_me] = send_b[...]

    for i in (7, 8, 9):
        loads[i].wait()
    lf[:, 0:640] = dot(lift[...], exp[...]).astype(BF)
    lf[:, 640:960] = vol[...]

    def element_block(e):
        res = dot(lf[...], rhs[:, pl.ds(pl.multiple_of(e * 256, 256), 256)])
        x, ay = e // 4, e % 4
        for rhi in range(2):
            r = x * 8 + rhi * 4 + ay
            at = (pl.ds(r, 320, stride=ROWS), slice(None))
            sf[at] = sf[at] + res[:, rhi * 128 : rhi * 128 + 128]

    @pl.when(s > 0)
    def _():
        pltpu.make_async_copy(az_send.at[0], az_recv.at[0], hx_r.at[0]).wait()

    @pl.when(s < 7)
    def _():
        pltpu.make_async_copy(az_send.at[0], az_recv.at[0], hx_r.at[1]).wait()

    @pl.loop(0, 4)
    def _(x):
        element_block(x * 4 + 1)
        element_block(x * 4 + 2)

    pltpu.make_async_copy(part.at[pl.ds(0, 7)], recv_b.at[pl.ds(0, 7)], rb).wait()
    total = jnp.sum(recv_b[...].astype(F32), axis=0)
    own = weight_own * (total - target_own)
    own_f[...] = own
    sens[q_me] = own.astype(BF)
    for step in steps:
        pltpu.make_async_remote_copy(
            src_ref=sens.at[q_me], dst_ref=sens.at[q_me], send_sem=sc, recv_sem=rc,
            device_id=group_peer(step), device_id_type=MESH,
        ).start()
    swap = pltpu.make_async_remote_copy(
        src_ref=own_f, dst_ref=other_f, send_sem=sp, recv_sem=rp,
        device_id=((s + 1) - 2 * core, a), device_id_type=MESH)
    swap.start()

    w_hi, w_lo = halves(wsam_ref[...])
    w_lo2 = (wsam_ref[...] - w_hi.astype(F32) - w_lo.astype(F32)).astype(BF)
    w3 = jnp.concatenate([w_hi, w_lo, w_lo2], axis=0)
    g_rows = [jnp.sum(dot(w3, ret[b]), axis=0, keepdims=True) for b in range(16)]
    g_hi, g_lo = halves(jnp.concatenate(g_rows, axis=0))
    gg = jnp.concatenate([g_hi, g_lo], axis=0)
    blank = jnp.zeros((32, 64), BF)
    g0[...] = jnp.concatenate([gg, blank], axis=1)
    g1[...] = jnp.concatenate([blank, gg], axis=1)
    host = host_ref[...]
    lo = host % 128
    oh_lo[...] = jnp.where(lax.broadcasted_iota(jnp.int32, (128, 2048), 0) == lo, 1.0, 0.0).astype(BF)
    hi = host // 128
    point_row = (hi // 8) * 8 + (hi % 2) * 4 + (hi // 2) % 4

    az_up.wait()
    az_dn.wait()
    for x in range(4):
        for rhi in range(2):
            src = slice(x * 256 + rhi * 128, x * 256 + rhi * 128 + 128)
            up = az_recv[0, :, src].astype(F32).reshape(10, 8, 128)
            even = jnp.concatenate([up[:, 4:8], up[:, 0:4]], axis=1)
            both = jnp.concatenate([even[:, None], up[:, None]], axis=1)
            c0 = (x * 8 + rhi) * 128
            rhs[160:320, c0 : c0 + 128] = both.reshape(160, 128).astype(BF)
            dn = az_recv[1, :, src].astype(F32).reshape(10, 8, 128)
            odd = jnp.concatenate([dn[:, 4:8], dn[:, 0:4]], axis=1)
            both = jnp.concatenate([dn[:, None], odd[:, None]], axis=1)
            c3 = (x * 8 + 6 + rhi) * 128
            rhs[320:480, c3 : c3 + 128] = both.reshape(160, 128).astype(BF)

    @pl.loop(0, 4)
    def _(x):
        element_block(x * 4)
        element_block(x * 4 + 3)

    out = pltpu.make_async_copy(sf, base_hbm, out_sem)
    out.start()

    pltpu.make_async_copy(sens.at[pl.ds(0, 31)], sens.at[pl.ds(0, 31)], rc).wait()
    flat = sens[...].reshape(512, 128)
    h_low = []
    for g in (g0, g1):
        h = dot(g[...], flat, NT)
        h_low.append(jnp.concatenate(halves(h[0:16] + h[16:32]), axis=0))
    block_of = lax.broadcasted_iota(jnp.int32, (32, 512), 0) % 16
    es = jnp.zeros((64, 128), F32)
    for n in range(4):
        cols = slice(n * 512, n * 512 + 512)
        val = dot(h_low[0], rad[:, 0, :, cols].reshape(512, 512))
        val = val + dot(h_low[1], rad[:, 1, :, cols].reshape(512, 512))
        mine = lax.broadcasted_iota(jnp.int32, (32, 512), 1) // 128 + n * 4 == block_of
        strength = jnp.sum(jnp.where(mine, val, 0.0), axis=0, keepdims=True)
        rows = lax.broadcasted_iota(jnp.int32, (32, 512), 0)
        spread_rows = jnp.where(rows == point_row[:, cols], strength, 0.0)
        pieces = jnp.concatenate(halves(spread_rows), axis=0)
        es = es + dot(pieces, oh_lo[:, cols], NT)
    es_ref[...] = es[0:32] + es[32:64]

    swap.wait()
    mine_f = jnp.where(core == z_hi, own_f[...], other_f[...])
    obs_ref[0:16, :] = mine_f[:, 0:64]
    obs_ref[16:32, :] = mine_f[:, 64:128]

    pltpu.make_async_copy(part.at[pl.ds(0, 31)], recv_a.at[pl.ds(0, 31)], sa).wait()
    pltpu.make_async_copy(part.at[pl.ds(0, 7)], recv_b.at[pl.ds(0, 7)], sb).wait()
    pltpu.make_async_copy(sens.at[pl.ds(0, 31)], sens.at[pl.ds(0, 31)], sc).wait()

    @pl.when(s < 7)
    def _():
        pltpu.make_async_copy(az_send.at[0], az_recv.at[0], hx_s.at[0]).wait()

    @pl.when(s > 0)
    def _():
        pltpu.make_async_copy(az_send.at[0], az_recv.at[0], hx_s.at[1]).wait()

    out.wait()


def hann_taper(count):
    samples = np.arange(count, dtype=np.float32)
    return (0.5 - 0.5 * np.cos(2.0 * np.pi * (samples + 0.5) / count)).astype(np.float32)


def body(
    surface_signal, retarded_weights, radiation_weights, target_signal, observer_weights,
    sample_weights, host_element, source_profile, adjoint_state, volume_operator, lift_operator,
):
    dma = pltpu.SemaphoreType.DMA
    state = adjoint_state.reshape(320, 4, 4, 2, 128).transpose(0, 1, 3, 2, 4).reshape(320, 32, 128)
    taper = jnp.asarray(np.repeat(hann_taper(64)[:, None], 128, axis=1))
    expand = jnp.asarray(expander(), dtype=BF)
    base, obs_t, es = pl.pallas_call(
        kernel,
        out_shape=(
            jax.ShapeDtypeStruct((10240, 128), F32),
            jax.ShapeDtypeStruct((32, 64), F32),
            jax.ShapeDtypeStruct((32, 128), F32),
        ),
        in_specs=[ANY] * 8 + [VM] * 4,
        out_specs=(ANY, VM, VM),
        scratch_shapes=[
            pltpu.VMEM((64, 2048), BF),
            pltpu.VMEM((16, 64, 64), BF),
            pltpu.VMEM((32, 2, 16, 2048), BF),
            pltpu.VMEM((320, 32, 128), BF),
            pltpu.VMEM((320, 480), BF),
            pltpu.VMEM((320, 320), BF),
            pltpu.VMEM((480, 640), BF),
            pltpu.VMEM((64, 1024), F32),
            pltpu.VMEM((128, 2048), BF),
            pltpu.VMEM((128, 2048), BF),
            pltpu.VMEM((32, 128), BF),
            pltpu.VMEM((32, 128), BF),
            pltpu.VMEM((32, 16, 128), BF),
            pltpu.VMEM((32, 16, 128), BF),
            pltpu.VMEM((16, 128), BF),
            pltpu.VMEM((8, 16, 128), BF),
            pltpu.VMEM((32, 16, 128), BF),
            pltpu.VMEM((16, 128), F32),
            pltpu.VMEM((16, 128), F32),
            pltpu.VMEM((10240, 128), F32),
            pltpu.VMEM((960, 4096), BF),
            pltpu.VMEM((320, 960), BF),
            pltpu.VMEM((2, 80, 1024), BF),
            pltpu.VMEM((2, 80, 1024), BF),
            pltpu.VMEM((128, 2048), BF),
            pltpu.VMEM((128, 64), F32),
            dma((11,)),
            dma, dma, dma, dma, dma, dma, dma, dma, dma,
            dma((2,)), dma((2,)), dma((2,)), dma((2,)),
        ],
        compiler_params=pltpu.CompilerParams(
            collective_id=0, has_side_effects=True, vmem_limit_bytes=48 * 1024 * 1024
        ),
    )(
        surface_signal,
        retarded_weights,
        radiation_weights.reshape(32, 2, 16, 2048),
        state,
        lift_operator,
        volume_operator,
        expand,
        target_signal,
        taper,
        observer_weights.reshape(1, 1024),
        sample_weights.reshape(1, 64),
        host_element.reshape(1, 2048),
    )
    updated = base.reshape(320, 32, 128) + source_profile[:, None, None] * es[None]
    updated = updated.reshape(320, 4, 2, 4, 128).transpose(0, 1, 3, 2, 4)
    return (obs_t.T, updated.reshape(320, 4, 4, 256))


def solution(mesh):
    return jax.shard_map(
        body,
        mesh=mesh,
        in_specs=(
            P(None, ("stream", "azim")),
            P(("stream", "azim"), None, None),
            P(None, ("stream", "azim")),
            P(),
            P(),
            P(),
            P(("stream", "azim")),
            P(),
            P(None, "stream", "azim", None),
            P(),
            P(),
        ),
        out_specs=(P(None, "azim"), P(None, "stream", "azim", None)),
        check_vma=False,
    )
```

```python
import jax
import jax.numpy as jnp
import numpy as np
from jax import lax
from jax.experimental import pallas as pl
from jax.experimental.pallas import tpu as pltpu
from jax.sharding import PartitionSpec as P

MESH = pl.DeviceIdType.MESH
BF = jnp.bfloat16
F32 = jnp.float32
ANY = pl.BlockSpec(memory_space=pl.ANY)
VM = pl.BlockSpec(memory_space=pltpu.VMEM)
FINISH = 10
ROWS = 32
PITCH = 33
FACE_PITCH = 9
NT = (((1,), (1,)), ((), ()))
TN = (((0,), (0,)), ((), ()))


def dot(a, b, dims=(((1,), (0,)), ((), ()))):
    return lax.dot_general(a, b, dims, preferred_element_type=F32)


def halves(x):
    top = x.astype(BF)
    return top, (x - top.astype(F32)).astype(BF)


def peers_by_distance():
    def hops(d):
        return min(d, 4 - d)

    steps = [(dx, dy, dc) for dx in range(4) for dy in range(4) for dc in range(2)]
    steps = [s for s in steps if s != (0, 0, 0)]
    return sorted(steps, key=lambda s: -(hops(s[0]) + hops(s[1])))


def expander():
    e = np.zeros((480, 640), np.float32)
    for j in range(160):
        e[j, j] = 1.0
    for vp in range(20):
        for w in range(4):
            e[160 + vp * 4 + w, 160 + vp * 8 + 4 + w] = 1.0
            e[240 + vp * 4 + w, 320 + vp * 8 + w] = 1.0
    for j in range(160):
        e[320 + j, 480 + j] = 1.0
    return e


def kernel(
    sig_hbm, ret_hbm, rad_hbm, state_hbm, lift_hbm, vol_hbm, exp_hbm, target_hbm,
    taper_hbm, wobs_hbm, wsam_hbm, host_hbm,
    sf, obs_ref, es_ref,
    sig, ret, rad, st, lift, vol, exp, target,
    d0, d1, g0, g1, part, recv_a, send_b, recv_b, sens, own_f, other_f,
    rhs, lf, az_send, az_recv, ax_recv, axf, oh_lo, tcol,
    taper_ref, wobs_ref, wsam_ref, host_ref,
    ld, sa, ra, sb, rb, sc, rc, sp, rp, hx_s, hx_r, ha_s, ha_r,
):
    s = lax.axis_index("stream")
    a = lax.axis_index("azim")
    core = s % 2
    z_lo = s // 2
    xy = a % 16
    z_hi = a // 16
    cx, cy = xy // 4, xy % 4
    q_me = core * 16 + xy
    z_me = z_hi * 4 + z_lo
    steps = peers_by_distance()
    planar = [(dx, dy) for dx, dy, dc in steps if dc == 1]

    def group_peer(step):
        dx, dy, dc = step
        return z_lo * 2 + (core + dc) % 2, z_hi * 16 + ((cx + dx) % 4) * 4 + (cy + dy) % 4

    def z_peer(dz):
        z = (z_me + dz) % 8
        return (z % 4) * 2 + core, (z // 4) * 16 + xy

    def q_of(peer):
        return (peer[0] % 2) * 16 + peer[1] % 16

    a_next, a_prev = (a + 1) % 32, (a + 31) % 32

    loads = {}

    def load(i, src, dst):
        loads[i] = pltpu.make_async_copy(src, dst, ld.at[i])
        loads[i].start()

    load(0, ret_hbm, ret)
    load(1, sig_hbm, sig)
    for c in range(4):
        load(2 + c, rad_hbm.at[pl.ds(c * 8, 8)], rad.at[pl.ds(c * 8, 8)])
    load(6, state_hbm, st)
    load(7, lift_hbm, lift)
    load(8, exp_hbm, exp)
    load(9, vol_hbm, vol)
    load(10, target_hbm, target)
    load(11, taper_hbm, taper_ref)
    load(12, wobs_hbm, wobs_ref)
    load(13, wsam_hbm, wsam_ref)
    load(14, host_hbm, host_ref)

    barrier = pltpu.get_barrier_semaphore()

    def greet(peer):
        pl.semaphore_signal(barrier, inc=1, device_id=peer, device_id_type=MESH)

    for step in steps:
        greet(group_peer(step))
    for dz in range(1, 8):
        greet(z_peer(dz))
    greet((s, a_next))
    greet((s, a_prev))

    @pl.when(s > 0)
    def _():
        greet((s - 1, a))

    @pl.when(s < 7)
    def _():
        greet((s + 1, a))

    loads[0].wait()
    loads[1].wait()
    d0[64:128, :] = jnp.zeros((64, 2048), BF)
    d1[0:64, :] = jnp.zeros((64, 2048), BF)
    for b in range(16):
        cols = slice(b * 128, b * 128 + 128)
        blk = dot(ret[b], sig[:, cols], TN).astype(BF)
        d0[0:64, cols] = blk
        d1[64:128, cols] = blk
    extra = jnp.where(s > 0, 1, 0) + jnp.where(s < 7, 1, 0)

    def send_partial(peer):
        pltpu.make_async_remote_copy(
            src_ref=part.at[q_of(peer)], dst_ref=recv_a.at[q_me], send_sem=sa, recv_sem=ra,
            device_id=peer, device_id_type=MESH,
        ).start()

    for g in range(2):
        q0 = g * 16
        loads[2 + 2 * g].wait()
        loads[3 + 2 * g].wait()
        acc = dot(rad[q0 : q0 + 16, 0].reshape(256, 2048), d0[...], NT)
        acc = acc + dot(rad[q0 : q0 + 16, 1].reshape(256, 2048), d1[...], NT)
        part[q0 : q0 + 16] = acc.reshape(16, 16, 128).astype(BF)
        if g == 0:
            pl.semaphore_wait(barrier, 40 + extra)
        for dx, dy in planar:
            peer = (z_lo * 2 + g, z_hi * 16 + ((cx + dx) % 4) * 4 + (cy + dy) % 4)
            if (dx, dy) != (0, 0):
                send_partial(peer)
            else:

                @pl.when(core != g)
                def _():
                    send_partial(peer)

    @pl.when(s < 7)
    def _():
        for v in range(5):
            pltpu.make_async_remote_copy(
                src_ref=state_hbm.at[pl.ds(v * 64 + 48, 16), pl.ds(24, 8)],
                dst_ref=ax_recv.at[0, pl.ds(v * 16, 16)],
                send_sem=hx_s.at[0], recv_sem=hx_r.at[0],
                device_id=(s + 1, a), device_id_type=MESH).start()

    @pl.when(s > 0)
    def _():
        for v in range(5):
            pltpu.make_async_remote_copy(
                src_ref=state_hbm.at[pl.ds(v * 64, 16), pl.ds(0, 8)],
                dst_ref=ax_recv.at[1, pl.ds(v * 16, 16)],
                send_sem=hx_s.at[1], recv_sem=hx_r.at[1],
                device_id=(s - 1, a), device_id_type=MESH).start()

    recv_a[q_me] = part[q_me]

    loads[6].wait()

    @pl.loop(0, 40)
    def _(i):
        for j in range(8):
            c = i * 8 + j
            sf[pl.ds(c * PITCH, ROWS), :] = st[c].astype(F32)

    lane = lax.broadcasted_iota(jnp.int32, (80, 128), 1)

    @pl.loop(0, 4)
    def _(x):
        for ay in range(4):
            roll_up, roll_dn = [], []
            for rhi in range(2):
                r = x * 8 + rhi * 4 + ay
                col = pl.multiple_of(x * 256 + rhi * 128, 128)
                f = sf[pl.ds(r, 320, stride=PITCH), :]
                xb = f.astype(BF)
                rhs[ay, 640:960, pl.ds(col, 128)] = xb
                x5 = xb.reshape(5, 64, 128)

                @pl.when(x < 3)
                def _():
                    rhs[ay, 0:80, pl.ds(col + 256, 128)] = x5[:, 48:64].reshape(80, 128)

                @pl.when(x > 0)
                def _():
                    rhs[ay, 80:160, pl.ds(col - 256, 128)] = x5[:, 0:16].reshape(80, 128)

                tiles = f.reshape(20, 2, 8, 128)
                upper = tiles[:, 1]
                lower = tiles[:, 0]
                if ay < 3:
                    rhs[ay + 1, 160:320, pl.ds(col, 128)] = upper.reshape(160, 128).astype(BF)
                else:
                    u = upper.reshape(10, 2, 8, 128)
                    packed = jnp.concatenate([u[:, 0, 4:8], u[:, 1, 4:8]], axis=1)
                    az_send[0, :, pl.ds(col, 128)] = packed.reshape(80, 128).astype(BF)
                if ay > 0:
                    rhs[ay - 1, 320:480, pl.ds(col, 128)] = lower.reshape(160, 128).astype(BF)
                else:
                    u = lower.reshape(10, 2, 8, 128)
                    packed = jnp.concatenate([u[:, 0, 0:4], u[:, 1, 0:4]], axis=1)
                    az_send[1, :, pl.ds(col, 128)] = packed.reshape(80, 128).astype(BF)
                roll_up.append(pltpu.roll(sf[pl.ds(3 * PITCH + r, 80, stride=4 * PITCH), :], 1, 1))
                roll_dn.append(pltpu.roll(sf[pl.ds(r, 80, stride=4 * PITCH), :], 127, 1))
            col = pl.multiple_of(x * 256, 256)
            zero = jnp.zeros((80, 128), F32)
            rhs[ay, 480:560, pl.ds(col, 128)] = jnp.where(lane == 0, zero, roll_up[0]).astype(BF)
            rhs[ay, 480:560, pl.ds(col + 128, 128)] = jnp.where(lane == 0, roll_up[0], roll_up[1]).astype(BF)
            rhs[ay, 560:640, pl.ds(col, 128)] = jnp.where(lane == 127, roll_dn[1], roll_dn[0]).astype(BF)
            rhs[ay, 560:640, pl.ds(col + 128, 128)] = jnp.where(lane == 127, zero, roll_dn[1]).astype(BF)

    az_up = pltpu.make_async_remote_copy(
        src_ref=az_send.at[0], dst_ref=az_recv.at[0], send_sem=ha_s.at[0], recv_sem=ha_r.at[0],
        device_id=(s, a_next), device_id_type=MESH)
    az_dn = pltpu.make_async_remote_copy(
        src_ref=az_send.at[1], dst_ref=az_recv.at[1], send_sem=ha_s.at[1], recv_sem=ha_r.at[1],
        device_id=(s, a_prev), device_id_type=MESH)
    az_up.start()
    az_dn.start()

    @pl.when(s == 0)
    def _():
        rhs[:, 0:80, 0:256] = jnp.zeros((4, 80, 256), BF)

    @pl.when(s == 7)
    def _():
        rhs[:, 80:160, 768:1024] = jnp.zeros((4, 80, 256), BF)

    for i in (10, 11, 12, 13, 14):
        loads[i].wait()
    kb = pl.multiple_of((q_me // 4) * 128, 128)
    row = pl.multiple_of((q_me % 4) * 32, 32)

    def packed_columns(block):
        tcol[...] = jnp.transpose(block)
        return jnp.concatenate(
            [tcol[pl.ds(row, 16), :], tcol[pl.ds(pl.multiple_of(row + 16, 16), 16), :]], axis=1)

    target_own = packed_columns(target[:, pl.ds(kb, 128)])
    weight_own = packed_columns(taper_ref[...] * wobs_ref[:, pl.ds(kb, 128)])

    pltpu.make_async_copy(part.at[pl.ds(0, 31)], recv_a.at[pl.ds(0, 31)], ra).wait()
    send_b[...] = jnp.sum(recv_a[...].astype(F32), axis=0).astype(BF)
    for dz in (4, 3, 5, 2, 6, 1, 7):
        pltpu.make_async_remote_copy(
            src_ref=send_b, dst_ref=recv_b.at[z_me], send_sem=sb, recv_sem=rb,
            device_id=z_peer(dz), device_id_type=MESH,
        ).start()
    recv_b[z_me] = send_b[...]

    for i in (7, 8, 9):
        loads[i].wait()
    lf[:, 0:640] = dot(lift[...], exp[...]).astype(BF)
    lf[:, 640:960] = vol[...]

    def sector_row(ay):
        res = dot(lf[...], rhs[ay])
        for x in range(4):
            for rhi in range(2):
                at = (pl.ds(x * 8 + rhi * 4 + ay, 320, stride=PITCH), slice(None))
                col = x * 256 + rhi * 128
                sf[at] = sf[at] + res[:, col : col + 128]

    def axial_halo(side, row, col):
        pltpu.make_async_copy(az_send.at[0], az_recv.at[0], hx_r.at[side]).wait()
        for c in range(80):
            axf[c * FACE_PITCH : c * FACE_PITCH + 8, :] = ax_recv[side, c].astype(F32)
        for rhi in range(2):
            for ay in range(4):
                face = axf[pl.ds(rhi * 4 + ay, 80, stride=FACE_PITCH), :].astype(BF)
                rhs[ay, row : row + 80, col + rhi * 128 : col + rhi * 128 + 128] = face

    @pl.when(s > 0)
    def _():
        axial_halo(0, 0, 0)

    @pl.when(s < 7)
    def _():
        axial_halo(1, 80, 768)

    @pl.loop(1, 3)
    def _(ay):
        sector_row(ay)

    pltpu.make_async_copy(part.at[pl.ds(0, 7)], recv_b.at[pl.ds(0, 7)], rb).wait()
    total = jnp.sum(recv_b[...].astype(F32), axis=0)
    own = weight_own * (total - target_own)
    own_f[...] = own
    sens[q_me] = own.astype(BF)
    for step in steps:
        pltpu.make_async_remote_copy(
            src_ref=sens.at[q_me], dst_ref=sens.at[q_me], send_sem=sc, recv_sem=rc,
            device_id=group_peer(step), device_id_type=MESH,
        ).start()
    swap = pltpu.make_async_remote_copy(
        src_ref=own_f, dst_ref=other_f, send_sem=sp, recv_sem=rp,
        device_id=((s + 1) - 2 * core, a), device_id_type=MESH)
    swap.start()

    w_hi, w_lo = halves(wsam_ref[...])
    w_lo2 = (wsam_ref[...] - w_hi.astype(F32) - w_lo.astype(F32)).astype(BF)
    w3 = jnp.concatenate([w_hi, w_lo, w_lo2], axis=0)
    g_rows = [jnp.sum(dot(w3, ret[b]), axis=0, keepdims=True) for b in range(16)]
    g_hi, g_lo = halves(jnp.concatenate(g_rows, axis=0))
    gg = jnp.concatenate([g_hi, g_lo], axis=0)
    blank = jnp.zeros((32, 64), BF)
    g0[...] = jnp.concatenate([gg, blank], axis=1)
    g1[...] = jnp.concatenate([blank, gg], axis=1)
    host = host_ref[...]
    lo = host % 128
    oh_lo[...] = jnp.where(lax.broadcasted_iota(jnp.int32, (128, 2048), 0) == lo, 1.0, 0.0).astype(BF)
    hi = host // 128
    point_row = (hi // 8) * 8 + (hi % 2) * 4 + (hi // 2) % 4

    az_up.wait()
    az_dn.wait()
    for x in range(4):
        for rhi in range(2):
            src = slice(x * 256 + rhi * 128, x * 256 + rhi * 128 + 128)
            up = az_recv[0, :, src].astype(F32).reshape(10, 8, 128)
            even = jnp.concatenate([up[:, 4:8], up[:, 0:4]], axis=1)
            both = jnp.concatenate([even[:, None], up[:, None]], axis=1)
            rhs[0, 160:320, src] = both.reshape(160, 128).astype(BF)
            dn = az_recv[1, :, src].astype(F32).reshape(10, 8, 128)
            odd = jnp.concatenate([dn[:, 4:8], dn[:, 0:4]], axis=1)
            both = jnp.concatenate([dn[:, None], odd[:, None]], axis=1)
            rhs[3, 320:480, src] = both.reshape(160, 128).astype(BF)

    @pl.loop(0, 2)
    def _(i):
        sector_row(i * 3)

    pltpu.make_async_copy(sens.at[pl.ds(0, 31)], sens.at[pl.ds(0, 31)], rc).wait()
    flat = sens[...].reshape(512, 128)
    h_low = []
    for g in (g0, g1):
        h = dot(g[...], flat, NT)
        h_low.append(jnp.concatenate(halves(h[0:16] + h[16:32]), axis=0))
    block_of = lax.broadcasted_iota(jnp.int32, (32, 512), 0) % 16
    es = jnp.zeros((64, 128), F32)
    for n in range(4):
        cols = slice(n * 512, n * 512 + 512)
        val = dot(h_low[0], rad[:, 0, :, cols].reshape(512, 512))
        val = val + dot(h_low[1], rad[:, 1, :, cols].reshape(512, 512))
        mine = lax.broadcasted_iota(jnp.int32, (32, 512), 1) // 128 + n * 4 == block_of
        strength = jnp.sum(jnp.where(mine, val, 0.0), axis=0, keepdims=True)
        rows = lax.broadcasted_iota(jnp.int32, (32, 512), 0)
        spread_rows = jnp.where(rows == point_row[:, cols], strength, 0.0)
        pieces = jnp.concatenate(halves(spread_rows), axis=0)
        es = es + dot(pieces, oh_lo[:, cols], NT)
    es_ref[...] = es[0:32] + es[32:64]

    swap.wait()
    mine_f = jnp.where(core == z_hi, own_f[...], other_f[...])
    obs_ref[0:16, :] = mine_f[:, 0:64]
    obs_ref[16:32, :] = mine_f[:, 64:128]

    pltpu.make_async_copy(part.at[pl.ds(0, 31)], recv_a.at[pl.ds(0, 31)], sa).wait()
    pltpu.make_async_copy(part.at[pl.ds(0, 7)], recv_b.at[pl.ds(0, 7)], sb).wait()
    pltpu.make_async_copy(sens.at[pl.ds(0, 31)], sens.at[pl.ds(0, 31)], sc).wait()

    @pl.when(s < 7)
    def _():
        pltpu.make_async_copy(az_send.at[0], az_recv.at[0], hx_s.at[0]).wait()

    @pl.when(s > 0)
    def _():
        pltpu.make_async_copy(az_send.at[0], az_recv.at[0], hx_s.at[1]).wait()


def finish(base_ref, es_ref, prof_ref, obs_in, out_hbm, obs_out, buf, sems):
    obs_out[...] = obs_in[...]
    es = es_ref[...]
    copies = []
    for k in range(FINISH):
        n = 320 // FINISH

        @pl.loop(0, n // 8)
        def _(i):
            for j in range(8):
                c = k * n + i * 8 + j
                rows = pl.ds(pl.multiple_of(c * ROWS, ROWS), ROWS)
                buf[rows, :] = base_ref[pl.ds(c * PITCH, ROWS), :] + prof_ref[c] * es

        part = pl.ds(k * n * ROWS, n * ROWS)
        copies.append(pltpu.make_async_copy(buf.at[part], out_hbm.at[part], sems.at[k]))
        copies[-1].start()
    for c in copies:
        c.wait()


def hann_taper(count):
    samples = np.arange(count, dtype=np.float32)
    return (0.5 - 0.5 * np.cos(2.0 * np.pi * (samples + 0.5) / count)).astype(np.float32)


def body(
    surface_signal, retarded_weights, radiation_weights, target_signal, observer_weights,
    sample_weights, host_element, source_profile, adjoint_state, volume_operator, lift_operator,
):
    dma = pltpu.SemaphoreType.DMA
    state = adjoint_state.reshape(320, 4, 4, 2, 128).transpose(0, 1, 3, 2, 4).reshape(320, 32, 128)
    taper = jnp.asarray(np.repeat(hann_taper(64)[:, None], 128, axis=1))
    expand = jnp.asarray(expander(), dtype=BF)
    base, obs_t, es = pl.pallas_call(
        kernel,
        out_shape=(
            pltpu.VMEM((320 * PITCH, 128), F32),
            jax.ShapeDtypeStruct((32, 64), F32),
            jax.ShapeDtypeStruct((32, 128), F32),
        ),
        in_specs=[ANY] * 12,
        out_specs=(VM, VM, VM),
        scratch_shapes=[
            pltpu.VMEM((64, 2048), BF),
            pltpu.VMEM((16, 64, 64), BF),
            pltpu.VMEM((32, 2, 16, 2048), BF),
            pltpu.VMEM((320, 32, 128), BF),
            pltpu.VMEM((320, 480), BF),
            pltpu.VMEM((320, 320), BF),
            pltpu.VMEM((480, 640), BF),
            pltpu.VMEM((64, 1024), F32),
            pltpu.VMEM((128, 2048), BF),
            pltpu.VMEM((128, 2048), BF),
            pltpu.VMEM((32, 128), BF),
            pltpu.VMEM((32, 128), BF),
            pltpu.VMEM((32, 16, 128), BF),
            pltpu.VMEM((32, 16, 128), BF),
            pltpu.VMEM((16, 128), BF),
            pltpu.VMEM((8, 16, 128), BF),
            pltpu.VMEM((32, 16, 128), BF),
            pltpu.VMEM((16, 128), F32),
            pltpu.VMEM((16, 128), F32),
            pltpu.VMEM((4, 960, 1024), BF),
            pltpu.VMEM((320, 960), BF),
            pltpu.VMEM((2, 80, 1024), BF),
            pltpu.VMEM((2, 80, 1024), BF),
            pltpu.VMEM((2, 80, 8, 128), BF),
            pltpu.VMEM((80 * FACE_PITCH, 128), F32),
            pltpu.VMEM((128, 2048), BF),
            pltpu.VMEM((128, 64), F32),
            pltpu.VMEM((64, 128), F32),
            pltpu.VMEM((1, 1024), F32),
            pltpu.VMEM((1, 64), F32),
            pltpu.VMEM((1, 2048), jnp.int32),
            dma((15,)),
            dma, dma, dma, dma, dma, dma, dma, dma,
            dma((2,)), dma((2,)), dma((2,)), dma((2,)),
        ],
        compiler_params=pltpu.CompilerParams(
            collective_id=0, has_side_effects=True, vmem_limit_bytes=48 * 1024 * 1024
        ),
    )(
        *(
            pltpu.with_memory_space_constraint(x, pltpu.HBM)
            for x in (
                surface_signal,
                retarded_weights,
                radiation_weights.reshape(32, 2, 16, 2048),
                state,
                lift_operator,
                volume_operator,
                expand,
                target_signal,
                taper,
                observer_weights.reshape(1, 1024),
                sample_weights.reshape(1, 64),
                host_element.reshape(1, 2048),
            )
        )
    )
    updated, obs_t = pl.pallas_call(
        finish,
        out_shape=(
            jax.ShapeDtypeStruct((10240, 128), F32),
            jax.ShapeDtypeStruct((32, 64), F32),
        ),
        in_specs=[VM, VM, pl.BlockSpec(memory_space=pltpu.SMEM), VM],
        out_specs=(ANY, VM),
        scratch_shapes=[pltpu.VMEM((10240, 128), F32), dma((FINISH,))],
        compiler_params=pltpu.CompilerParams(vmem_limit_bytes=16 * 1024 * 1024),
    )(pltpu.with_memory_space_constraint(base, pltpu.VMEM), es, source_profile, obs_t)
    updated = updated.reshape(320, 4, 2, 4, 128).transpose(0, 1, 3, 2, 4)
    return (obs_t.T, updated.reshape(320, 4, 4, 256))


def solution(mesh):
    return jax.shard_map(
        body,
        mesh=mesh,
        in_specs=(
            P(None, ("stream", "azim")),
            P(("stream", "azim"), None, None),
            P(None, ("stream", "azim")),
            P(),
            P(),
            P(),
            P(("stream", "azim")),
            P(),
            P(None, "stream", "azim", None),
            P(),
            P(),
        ),
        out_specs=(P(None, "azim"), P(None, "stream", "azim", None)),
        check_vma=False,
    )
```

```python
import jax
import jax.numpy as jnp
import numpy as np
from jax import lax
from jax.experimental import pallas as pl
from jax.experimental.pallas import tpu as pltpu
from jax.sharding import PartitionSpec as P

MESH = pl.DeviceIdType.MESH
BF = jnp.bfloat16
F32 = jnp.float32
ANY = pl.BlockSpec(memory_space=pl.ANY)
VM = pl.BlockSpec(memory_space=pltpu.VMEM)
FINISH = 10
ROWS = 32
PITCH = 33
FACE_PITCH = 9
RELAYS = ((12, 3, 14, 11), (1, 4, 13, 7))
NT = (((1,), (1,)), ((), ()))
TN = (((0,), (0,)), ((), ()))


def dot(a, b, dims=(((1,), (0,)), ((), ()))):
    return lax.dot_general(a, b, dims, preferred_element_type=F32)


def halves(x):
    top = x.astype(BF)
    return top, (x - top.astype(F32)).astype(BF)


def peers_by_distance():
    def hops(d):
        return min(d, 4 - d)

    steps = [(dx, dy, dc) for dx in range(4) for dy in range(4) for dc in range(2)]
    steps = [s for s in steps if s != (0, 0, 0)]
    return sorted(steps, key=lambda s: -(hops(s[0]) + hops(s[1])))


def expander():
    e = np.zeros((480, 640), np.float32)
    for j in range(160):
        e[j, j] = 1.0
    for vp in range(20):
        for w in range(4):
            e[160 + vp * 4 + w, 160 + vp * 8 + 4 + w] = 1.0
            e[240 + vp * 4 + w, 320 + vp * 8 + w] = 1.0
    for j in range(160):
        e[320 + j, 480 + j] = 1.0
    return e


def kernel(
    sig_hbm, ret_hbm, rad_hbm, state_hbm, lift_hbm, vol_hbm, exp_hbm, target_hbm,
    taper_hbm, wobs_hbm, wsam_hbm, host_hbm, prof_hbm,
    sf, obs_ref, es_ref, prof_rows,
    sig, ret, rad, st, lift, vol, exp, target,
    d0, d1, g0, g1, part, recv_a, send_b, recv_b, sens, own_f, other_f,
    rhs, lf, az_send, az_recv, ax_recv, axf, oh_lo, tcol,
    taper_ref, wobs_ref, wsam_ref, host_ref, prof_ref, relay,
    ld, sa, ra, sb, rb, sc, rc, sp, rp, hx_s, hx_r, ha_s, ha_r, rel_s, rel_r,
):
    s = lax.axis_index("stream")
    a = lax.axis_index("azim")
    core = s % 2
    z_lo = s // 2
    xy = a % 16
    z_hi = a // 16
    cx, cy = xy // 4, xy % 4
    q_me = core * 16 + xy
    z_me = z_hi * 4 + z_lo
    steps = peers_by_distance()

    def group_peer(step):
        dx, dy, dc = step
        return z_lo * 2 + (core + dc) % 2, z_hi * 16 + ((cx + dx) % 4) * 4 + (cy + dy) % 4

    def z_peer(dz):
        z = (z_me + dz) % 8
        return (z % 4) * 2 + core, (z // 4) * 16 + xy

    def q_of(peer):
        return (peer[0] % 2) * 16 + peer[1] % 16

    a_next, a_prev = (a + 1) % 32, (a + 31) % 32

    loads = {}

    def load(i, src, dst):
        loads[i] = pltpu.make_async_copy(src, dst, ld.at[i])
        loads[i].start()

    load(0, ret_hbm, ret)
    load(1, sig_hbm, sig)
    for c in range(4):
        load(2 + c, rad_hbm.at[pl.ds(c * 8, 8)], rad.at[pl.ds(c * 8, 8)])

    def load_rest():
        load(6, state_hbm, st)
        load(7, lift_hbm, lift)
        load(8, exp_hbm, exp)
        load(9, vol_hbm, vol)
        load(10, target_hbm, target)
        load(11, taper_hbm, taper_ref)
        load(12, wobs_hbm, wobs_ref)
        load(13, wsam_hbm, wsam_ref)
        load(14, host_hbm, host_ref)
        load(15, prof_hbm, prof_ref)

    barrier = pltpu.get_barrier_semaphore()

    def greet(peer):
        pl.semaphore_signal(barrier, inc=1, device_id=peer, device_id_type=MESH)

    for step in steps:
        greet(group_peer(step))
    for dz in range(1, 8):
        greet(z_peer(dz))
    greet((s, a_next))
    greet((s, a_prev))

    @pl.when(s > 0)
    def _():
        greet((s - 1, a))

    @pl.when(s < 7)
    def _():
        greet((s + 1, a))

    ends = (15, 0)
    for way in range(2):
        for k in RELAYS[way]:

            @pl.when(xy == ends[1 - way])
            def _():
                greet((s, (1 - z_hi) * 16 + k))

    loads[0].wait()
    loads[1].wait()
    d0[64:128, :] = jnp.zeros((64, 2048), BF)
    d1[0:64, :] = jnp.zeros((64, 2048), BF)
    for b in range(16):
        cols = slice(b * 128, b * 128 + 128)
        blk = dot(ret[b], sig[:, cols], TN).astype(BF)
        d0[0:64, cols] = blk
        d1[64:128, cols] = blk
    extra = jnp.where(s > 0, 1, 0) + jnp.where(s < 7, 1, 0)
    for k in RELAYS[0] + RELAYS[1]:
        extra = extra + jnp.where(xy == k, 1, 0)

    def send_partial(peer):
        pltpu.make_async_remote_copy(
            src_ref=part.at[q_of(peer)], dst_ref=recv_a.at[q_me], send_sem=sa, recv_sem=ra,
            device_id=peer, device_id_type=MESH,
        ).start()

    for g in range(4):
        q0 = g * 8
        loads[2 + g].wait()
        acc = dot(rad[q0 : q0 + 8, 0].reshape(128, 2048), d0[...], NT)
        acc = acc + dot(rad[q0 : q0 + 8, 1].reshape(128, 2048), d1[...], NT)
        part[q0 : q0 + 8] = acc.reshape(8, 16, 128).astype(BF)
        if g == 0:
            pl.semaphore_wait(barrier, 40 + extra)
        if g == 2:
            load_rest()
        for dx in (1, 0):
            for dy in (2, 1, 3, 0):
                px, py = (g % 2) * 2 + (cx + dx) % 2, (cy + dy) % 4
                peer = (z_lo * 2 + g // 2, z_hi * 16 + px * 4 + py)
                if dy != 0:
                    send_partial(peer)
                else:

                    @pl.when(q_of(peer) != q_me)
                    def _():
                        send_partial(peer)

    @pl.when(s < 7)
    def _():
        for v in range(5):
            pltpu.make_async_remote_copy(
                src_ref=state_hbm.at[pl.ds(v * 64 + 48, 16), pl.ds(24, 8)],
                dst_ref=ax_recv.at[0, pl.ds(v * 16, 16)],
                send_sem=hx_s.at[0], recv_sem=hx_r.at[0],
                device_id=(s + 1, a), device_id_type=MESH).start()

    @pl.when(s > 0)
    def _():
        for v in range(5):
            pltpu.make_async_remote_copy(
                src_ref=state_hbm.at[pl.ds(v * 64, 16), pl.ds(0, 8)],
                dst_ref=ax_recv.at[1, pl.ds(v * 16, 16)],
                send_sem=hx_s.at[1], recv_sem=hx_r.at[1],
                device_id=(s - 1, a), device_id_type=MESH).start()

    recv_a[q_me] = part[q_me]

    loads[6].wait()

    @pl.loop(0, 40)
    def _(i):
        for j in range(8):
            c = i * 8 + j
            sf[pl.ds(c * PITCH, ROWS), :] = st[c].astype(F32)

    @pl.loop(0, 4)
    def _(x):
        for rhi in range(2):
            col = pl.multiple_of(x * 256 + rhi * 128, 128)
            last = sf[pl.ds(x * 8 + rhi * 4 + 3, 320, stride=PITCH), :].reshape(10, 2, 2, 8, 128)
            packed = jnp.concatenate([last[:, 0, 1, 4:8], last[:, 1, 1, 4:8]], axis=1)
            az_send[0, :, pl.ds(col, 128)] = packed.reshape(80, 128).astype(BF)
            first = sf[pl.ds(x * 8 + rhi * 4, 320, stride=PITCH), :].reshape(10, 2, 2, 8, 128)
            packed = jnp.concatenate([first[:, 0, 0, 0:4], first[:, 1, 0, 0:4]], axis=1)
            az_send[1, :, pl.ds(col, 128)] = packed.reshape(80, 128).astype(BF)

    def az_copy(way, dst):
        return pltpu.make_async_remote_copy(
            src_ref=az_send.at[way], dst_ref=az_recv.at[way], send_sem=ha_s.at[way],
            recv_sem=ha_r.at[way], device_id=(s, dst), device_id_type=MESH)

    az_up, az_dn = az_copy(0, a_next), az_copy(1, a_prev)
    for way, dst in ((0, a_next), (1, a_prev)):

        @pl.when(xy == ends[way])
        def _():
            for i, k in enumerate(RELAYS[way]):
                pltpu.make_async_remote_copy(
                    src_ref=az_send.at[way, pl.ds(16 * i + 16, 16)], dst_ref=relay,
                    send_sem=ha_s.at[way], recv_sem=rel_r,
                    device_id=(s, z_hi * 16 + k), device_id_type=MESH).start()
            first = pl.ds(0, 16)
            pltpu.make_async_remote_copy(
                src_ref=az_send.at[way, first], dst_ref=az_recv.at[way, first],
                send_sem=ha_s.at[way], recv_sem=ha_r.at[way],
                device_id=(s, dst), device_id_type=MESH).start()

    lane = lax.broadcasted_iota(jnp.int32, (80, 128), 1)

    @pl.loop(0, 4)
    def _(x):
        for ay in range(4):
            roll_up, roll_dn = [], []
            for rhi in range(2):
                r = x * 8 + rhi * 4 + ay
                col = pl.multiple_of(x * 256 + rhi * 128, 128)
                f = sf[pl.ds(r, 320, stride=PITCH), :]
                xb = f.astype(BF)
                rhs[ay, 640:960, pl.ds(col, 128)] = xb
                x5 = xb.reshape(5, 64, 128)

                @pl.when(x < 3)
                def _():
                    rhs[ay, 0:80, pl.ds(col + 256, 128)] = x5[:, 48:64].reshape(80, 128)

                @pl.when(x > 0)
                def _():
                    rhs[ay, 80:160, pl.ds(col - 256, 128)] = x5[:, 0:16].reshape(80, 128)

                tiles = f.reshape(20, 2, 8, 128)
                upper = tiles[:, 1]
                lower = tiles[:, 0]
                if ay < 3:
                    rhs[ay + 1, 160:320, pl.ds(col, 128)] = upper.reshape(160, 128).astype(BF)
                if ay > 0:
                    rhs[ay - 1, 320:480, pl.ds(col, 128)] = lower.reshape(160, 128).astype(BF)
                roll_up.append(pltpu.roll(sf[pl.ds(3 * PITCH + r, 80, stride=4 * PITCH), :], 1, 1))
                roll_dn.append(pltpu.roll(sf[pl.ds(r, 80, stride=4 * PITCH), :], 127, 1))
            col = pl.multiple_of(x * 256, 256)
            zero = jnp.zeros((80, 128), F32)
            rhs[ay, 480:560, pl.ds(col, 128)] = jnp.where(lane == 0, zero, roll_up[0]).astype(BF)
            rhs[ay, 480:560, pl.ds(col + 128, 128)] = jnp.where(lane == 0, roll_up[0], roll_up[1]).astype(BF)
            rhs[ay, 560:640, pl.ds(col, 128)] = jnp.where(lane == 127, roll_dn[1], roll_dn[0]).astype(BF)
            rhs[ay, 560:640, pl.ds(col + 128, 128)] = jnp.where(lane == 127, zero, roll_dn[1]).astype(BF)

    @pl.when(xy < 15)
    def _():
        az_up.start()

    @pl.when(xy > 0)
    def _():
        az_dn.start()

    @pl.when(s == 0)
    def _():
        rhs[:, 0:80, 0:256] = jnp.zeros((4, 80, 256), BF)

    @pl.when(s == 7)
    def _():
        rhs[:, 80:160, 768:1024] = jnp.zeros((4, 80, 256), BF)

    for i in (10, 11, 12, 13, 14, 15):
        loads[i].wait()
    for c0, c1 in ((0, 128), (128, 256), (256, 320)):
        line = prof_ref[c0:c1].reshape(1, c1 - c0)
        prof_rows[c0:c1, :] = jnp.transpose(jnp.broadcast_to(line, (128, c1 - c0)))
    kb = pl.multiple_of((q_me // 4) * 128, 128)
    row = pl.multiple_of((q_me % 4) * 32, 32)

    def packed_columns(block):
        tcol[...] = jnp.transpose(block)
        return jnp.concatenate(
            [tcol[pl.ds(row, 16), :], tcol[pl.ds(pl.multiple_of(row + 16, 16), 16), :]], axis=1)

    target_own = packed_columns(target[:, pl.ds(kb, 128)])
    weight_own = packed_columns(taper_ref[...] * wobs_ref[:, pl.ds(kb, 128)])

    pltpu.make_async_copy(part.at[pl.ds(0, 31)], recv_a.at[pl.ds(0, 31)], ra).wait()
    send_b[...] = jnp.sum(recv_a[...].astype(F32), axis=0).astype(BF)
    for dz in (4, 3, 5, 2, 6, 1, 7):
        pltpu.make_async_remote_copy(
            src_ref=send_b, dst_ref=recv_b.at[z_me], send_sem=sb, recv_sem=rb,
            device_id=z_peer(dz), device_id_type=MESH,
        ).start()
    recv_b[z_me] = send_b[...]

    def forward(way):
        for i, k in enumerate(RELAYS[way]):

            @pl.when(xy == k)
            def _():
                pltpu.make_async_copy(az_send.at[0, pl.ds(0, 16)], relay, rel_r).wait()
                rows = pl.ds(16 * i + 16, 16)
                pltpu.make_async_remote_copy(
                    src_ref=relay, dst_ref=az_recv.at[way, rows], send_sem=rel_s, recv_sem=ha_r.at[way],
                    device_id=(s, (1 - z_hi) * 16 + ends[1 - way]), device_id_type=MESH).start()

    forward(0)
    forward(1)

    for i in (7, 8, 9):
        loads[i].wait()
    lf[:, 0:640] = dot(lift[...], exp[...]).astype(BF)
    lf[:, 640:960] = vol[...]

    def sector_row(ay):
        res = dot(lf[...], rhs[ay])
        for x in range(4):
            for rhi in range(2):
                at = (pl.ds(x * 8 + rhi * 4 + ay, 320, stride=PITCH), slice(None))
                col = x * 256 + rhi * 128
                sf[at] = sf[at] + res[:, col : col + 128]

    def axial_halo(side, row, col):
        pltpu.make_async_copy(az_send.at[0], az_recv.at[0], hx_r.at[side]).wait()
        for c in range(80):
            axf[c * FACE_PITCH : c * FACE_PITCH + 8, :] = ax_recv[side, c].astype(F32)
        for rhi in range(2):
            for ay in range(4):
                face = axf[pl.ds(rhi * 4 + ay, 80, stride=FACE_PITCH), :].astype(BF)
                rhs[ay, row : row + 80, col + rhi * 128 : col + rhi * 128 + 128] = face

    @pl.when(s > 0)
    def _():
        axial_halo(0, 0, 0)

    @pl.when(s < 7)
    def _():
        axial_halo(1, 80, 768)

    @pl.loop(1, 3)
    def _(ay):
        sector_row(ay)

    pltpu.make_async_copy(part.at[pl.ds(0, 7)], recv_b.at[pl.ds(0, 7)], rb).wait()
    total = jnp.sum(recv_b[...].astype(F32), axis=0)
    own = weight_own * (total - target_own)
    own_f[...] = own
    sens[q_me] = own.astype(BF)
    for step in steps:
        pltpu.make_async_remote_copy(
            src_ref=sens.at[q_me], dst_ref=sens.at[q_me], send_sem=sc, recv_sem=rc,
            device_id=group_peer(step), device_id_type=MESH,
        ).start()
    swap = pltpu.make_async_remote_copy(
        src_ref=own_f, dst_ref=other_f, send_sem=sp, recv_sem=rp,
        device_id=((s + 1) - 2 * core, a), device_id_type=MESH)
    swap.start()

    w_hi, w_lo = halves(wsam_ref[...])
    w_lo2 = (wsam_ref[...] - w_hi.astype(F32) - w_lo.astype(F32)).astype(BF)
    w3 = jnp.concatenate([w_hi, w_lo, w_lo2], axis=0)
    g_rows = [jnp.sum(dot(w3, ret[b]), axis=0, keepdims=True) for b in range(16)]
    g_hi, g_lo = halves(jnp.concatenate(g_rows, axis=0))
    gg = jnp.concatenate([g_hi, g_lo], axis=0)
    blank = jnp.zeros((32, 64), BF)
    g0[...] = jnp.concatenate([gg, blank], axis=1)
    g1[...] = jnp.concatenate([blank, gg], axis=1)
    host = host_ref[...]
    lo = host % 128
    oh_lo[...] = jnp.where(lax.broadcasted_iota(jnp.int32, (128, 2048), 0) == lo, 1.0, 0.0).astype(BF)
    hi = host // 128
    point_row = (hi // 8) * 8 + (hi % 2) * 4 + (hi // 2) % 4

    az_up.wait()
    az_dn.wait()
    for x in range(4):
        for rhi in range(2):
            src = slice(x * 256 + rhi * 128, x * 256 + rhi * 128 + 128)
            up = az_recv[0, :, src].astype(F32).reshape(10, 8, 128)
            even = jnp.concatenate([up[:, 4:8], up[:, 0:4]], axis=1)
            both = jnp.concatenate([even[:, None], up[:, None]], axis=1)
            rhs[0, 160:320, src] = both.reshape(160, 128).astype(BF)
            dn = az_recv[1, :, src].astype(F32).reshape(10, 8, 128)
            odd = jnp.concatenate([dn[:, 4:8], dn[:, 0:4]], axis=1)
            both = jnp.concatenate([dn[:, None], odd[:, None]], axis=1)
            rhs[3, 320:480, src] = both.reshape(160, 128).astype(BF)

    @pl.loop(0, 2)
    def _(i):
        sector_row(i * 3)

    pltpu.make_async_copy(sens.at[pl.ds(0, 31)], sens.at[pl.ds(0, 31)], rc).wait()
    flat = sens[...].reshape(512, 128)
    h_low = []
    for g in (g0, g1):
        h = dot(g[...], flat, NT)
        h_low.append(jnp.concatenate(halves(h[0:16] + h[16:32]), axis=0))
    block_of = lax.broadcasted_iota(jnp.int32, (32, 512), 0) % 16
    es = jnp.zeros((64, 128), F32)
    for n in range(4):
        cols = slice(n * 512, n * 512 + 512)
        val = dot(h_low[0], rad[:, 0, :, cols].reshape(512, 512))
        val = val + dot(h_low[1], rad[:, 1, :, cols].reshape(512, 512))
        mine = lax.broadcasted_iota(jnp.int32, (32, 512), 1) // 128 + n * 4 == block_of
        strength = jnp.sum(jnp.where(mine, val, 0.0), axis=0, keepdims=True)
        rows = lax.broadcasted_iota(jnp.int32, (32, 512), 0)
        spread_rows = jnp.where(rows == point_row[:, cols], strength, 0.0)
        pieces = jnp.concatenate(halves(spread_rows), axis=0)
        es = es + dot(pieces, oh_lo[:, cols], NT)
    es_ref[...] = es[0:32] + es[32:64]

    swap.wait()
    mine_f = jnp.where(core == z_hi, own_f[...], other_f[...])
    obs_ref[0:16, :] = mine_f[:, 0:64]
    obs_ref[16:32, :] = mine_f[:, 64:128]

    pltpu.make_async_copy(part.at[pl.ds(0, 31)], recv_a.at[pl.ds(0, 31)], sa).wait()
    pltpu.make_async_copy(part.at[pl.ds(0, 7)], recv_b.at[pl.ds(0, 7)], sb).wait()
    pltpu.make_async_copy(sens.at[pl.ds(0, 31)], sens.at[pl.ds(0, 31)], sc).wait()

    @pl.when(s < 7)
    def _():
        pltpu.make_async_copy(az_send.at[0], az_recv.at[0], hx_s.at[0]).wait()

    @pl.when(s > 0)
    def _():
        pltpu.make_async_copy(az_send.at[0], az_recv.at[0], hx_s.at[1]).wait()

    for k in RELAYS[0] + RELAYS[1]:

        @pl.when(xy == k)
        def _():
            pltpu.make_async_copy(az_send.at[0, pl.ds(0, 16)], relay, rel_s).wait()


def finish(base_ref, es_ref, prof_ref, obs_in, out_hbm, obs_out, buf, sems):
    copies = [pltpu.make_async_copy(obs_in, obs_out, sems.at[FINISH])]
    copies[0].start()
    es = es_ref[...]
    for k in range(FINISH):
        n = 320 // FINISH

        @pl.loop(0, n // 8)
        def _(i):
            for j in range(8):
                c = k * n + i * 8 + j
                rows = pl.ds(pl.multiple_of(c * ROWS, ROWS), ROWS)
                buf[rows, :] = base_ref[pl.ds(c * PITCH, ROWS), :] + prof_ref[pl.ds(c, 1), :] * es

        part = pl.ds(k * n * ROWS, n * ROWS)
        copies.append(pltpu.make_async_copy(buf.at[part], out_hbm.at[part], sems.at[k]))
        copies[-1].start()
    for c in copies:
        c.wait()


def hann_taper(count):
    samples = np.arange(count, dtype=np.float32)
    return (0.5 - 0.5 * np.cos(2.0 * np.pi * (samples + 0.5) / count)).astype(np.float32)


def body(
    surface_signal, retarded_weights, radiation_weights, target_signal, observer_weights,
    sample_weights, host_element, source_profile, adjoint_state, volume_operator, lift_operator,
):
    dma = pltpu.SemaphoreType.DMA
    state = adjoint_state.reshape(320, 4, 4, 2, 128).transpose(0, 1, 3, 2, 4).reshape(320, 32, 128)
    taper = jnp.asarray(np.repeat(hann_taper(64)[:, None], 128, axis=1))
    expand = jnp.asarray(expander(), dtype=BF)
    base, obs_t, es, prof_rows = pl.pallas_call(
        kernel,
        out_shape=(
            pltpu.VMEM((320 * PITCH, 128), F32),
            jax.ShapeDtypeStruct((32, 64), F32),
            jax.ShapeDtypeStruct((32, 128), F32),
            pltpu.VMEM((320, 128), F32),
        ),
        in_specs=[ANY] * 13,
        out_specs=(VM, VM, VM, VM),
        scratch_shapes=[
            pltpu.VMEM((64, 2048), BF),
            pltpu.VMEM((16, 64, 64), BF),
            pltpu.VMEM((32, 2, 16, 2048), BF),
            pltpu.VMEM((320, 32, 128), BF),
            pltpu.VMEM((320, 480), BF),
            pltpu.VMEM((320, 320), BF),
            pltpu.VMEM((480, 640), BF),
            pltpu.VMEM((64, 1024), F32),
            pltpu.VMEM((128, 2048), BF),
            pltpu.VMEM((128, 2048), BF),
            pltpu.VMEM((32, 128), BF),
            pltpu.VMEM((32, 128), BF),
            pltpu.VMEM((32, 16, 128), BF),
            pltpu.VMEM((32, 16, 128), BF),
            pltpu.VMEM((16, 128), BF),
            pltpu.VMEM((8, 16, 128), BF),
            pltpu.VMEM((32, 16, 128), BF),
            pltpu.VMEM((16, 128), F32),
            pltpu.VMEM((16, 128), F32),
            pltpu.VMEM((4, 960, 1024), BF),
            pltpu.VMEM((320, 960), BF),
            pltpu.VMEM((2, 80, 1024), BF),
            pltpu.VMEM((2, 80, 1024), BF),
            pltpu.VMEM((2, 80, 8, 128), BF),
            pltpu.VMEM((80 * FACE_PITCH, 128), F32),
            pltpu.VMEM((128, 2048), BF),
            pltpu.VMEM((128, 64), F32),
            pltpu.VMEM((64, 128), F32),
            pltpu.VMEM((1, 1024), F32),
            pltpu.VMEM((1, 64), F32),
            pltpu.VMEM((1, 2048), jnp.int32),
            pltpu.VMEM((320,), F32),
            pltpu.VMEM((16, 1024), BF),
            dma((16,)),
            dma, dma, dma, dma, dma, dma, dma, dma,
            dma((2,)), dma((2,)), dma((2,)), dma((2,)), dma, dma,
        ],
        compiler_params=pltpu.CompilerParams(
            collective_id=0, has_side_effects=True, vmem_limit_bytes=48 * 1024 * 1024
        ),
    )(
        *(
            pltpu.with_memory_space_constraint(x, pltpu.HBM)
            for x in (
                surface_signal,
                retarded_weights,
                radiation_weights.reshape(32, 2, 16, 2048),
                state,
                lift_operator,
                volume_operator,
                expand,
                target_signal,
                taper,
                observer_weights.reshape(1, 1024),
                sample_weights.reshape(1, 64),
                host_element.reshape(1, 2048),
                source_profile,
            )
        )
    )
    updated, obs_t = pl.pallas_call(
        finish,
        out_shape=(
            jax.ShapeDtypeStruct((10240, 128), F32),
            jax.ShapeDtypeStruct((32, 64), F32),
        ),
        in_specs=[VM, VM, VM, VM],
        out_specs=(ANY, ANY),
        scratch_shapes=[pltpu.VMEM((10240, 128), F32), dma((FINISH + 1,))],
        compiler_params=pltpu.CompilerParams(vmem_limit_bytes=16 * 1024 * 1024),
    )(
        pltpu.with_memory_space_constraint(base, pltpu.VMEM),
        es,
        pltpu.with_memory_space_constraint(prof_rows, pltpu.VMEM),
        obs_t,
    )
    updated = updated.reshape(320, 4, 2, 4, 128).transpose(0, 1, 3, 2, 4)
    return (obs_t.T, updated.reshape(320, 4, 4, 256))


def solution(mesh):
    return jax.shard_map(
        body,
        mesh=mesh,
        in_specs=(
            P(None, ("stream", "azim")),
            P(("stream", "azim"), None, None),
            P(None, ("stream", "azim")),
            P(),
            P(),
            P(),
            P(("stream", "azim")),
            P(),
            P(None, "stream", "azim", None),
            P(),
            P(),
        ),
        out_specs=(P(None, "azim"), P(None, "stream", "azim", None)),
        check_vma=False,
    )
```

```python
import jax
import jax.numpy as jnp
import numpy as np
from jax import lax
from jax.experimental import pallas as pl
from jax.experimental.pallas import tpu as pltpu
from jax.sharding import PartitionSpec as P

MESH = pl.DeviceIdType.MESH
BF = jnp.bfloat16
F32 = jnp.float32
ANY = pl.BlockSpec(memory_space=pl.ANY)
VM = pl.BlockSpec(memory_space=pltpu.VMEM)
FINISH = 10
GREETED = 2
ROWS = 32
PITCH = 33
FACE_PITCH = 9
RELAYS = ((12, 3, 14, 11), (1, 4, 13, 7))
NT = (((1,), (1,)), ((), ()))
TN = (((0,), (0,)), ((), ()))


def dot(a, b, dims=(((1,), (0,)), ((), ()))):
    return lax.dot_general(a, b, dims, preferred_element_type=F32)


def halves(x):
    top = x.astype(BF)
    return top, (x - top.astype(F32)).astype(BF)


def peers_by_distance():
    def hops(d):
        return min(d, 4 - d)

    steps = [(dx, dy, dc) for dx in range(4) for dy in range(4) for dc in range(2)]
    steps = [s for s in steps if s != (0, 0, 0)]
    return sorted(steps, key=lambda s: -(hops(s[0]) + hops(s[1])))


def expander():
    e = np.zeros((480, 640), np.float32)
    for j in range(160):
        e[j, j] = 1.0
    for vp in range(20):
        for w in range(4):
            e[160 + vp * 4 + w, 160 + vp * 8 + 4 + w] = 1.0
            e[240 + vp * 4 + w, 320 + vp * 8 + w] = 1.0
    for j in range(160):
        e[320 + j, 480 + j] = 1.0
    return e


def kernel(
    sig_hbm, ret_hbm, rad_hbm, state_hbm, lift_hbm, vol_hbm, exp_hbm, target_hbm,
    taper_hbm, wobs_hbm, wsam_hbm, host_hbm, prof_hbm,
    sf, obs_ref, es_ref, prof_rows,
    sig, ret, rad, st, lift, vol, exp, target,
    d0, d1, g0, g1, part, recv_a, send_b, recv_b, sens, own_f, other_f,
    rhs, lf, az_send, az_recv, ax_recv, axf, oh_lo, tcol,
    taper_ref, wobs_ref, wsam_ref, host_ref, prof_ref, relay, first,
    ld, sa, ra, sb, rb, sc, rc, sp, rp, hx_s, hx_r, ha_s, ha_r, rel_s, rel_r,
):
    s = lax.axis_index("stream")
    a = lax.axis_index("azim")
    z_lo = s // 2
    core = s - z_lo * 2
    z_hi = a // 16
    xy = a - z_hi * 16
    cx = xy // 4
    cy = xy - cx * 4
    q_me = core * 16 + xy
    z_me = z_hi * 4 + z_lo
    steps = peers_by_distance()

    xs = [lax.rem(cx + d, 4) for d in range(4)]
    ys = [lax.rem(cy + d, 4) for d in range(4)]
    cs = [core, 1 - core]
    zs = [lax.rem(z_me + d, 8) for d in range(8)]
    own_z, own_half = z_lo * 2, z_hi * 16

    def group_peer(step):
        dx, dy, dc = step
        return own_z + cs[dc], own_half + xs[dx] * 4 + ys[dy]

    def z_peer(dz):
        half = zs[dz] // 4
        return (zs[dz] - half * 4) * 2 + core, half * 16 + xy

    a_next, a_prev = lax.rem(a + 1, 32), lax.rem(a + 31, 32)

    loads = {}

    def load(i, src, dst):
        loads[i] = pltpu.make_async_copy(src, dst, ld.at[i])
        loads[i].start()

    load(0, ret_hbm, ret)
    load(1, sig_hbm, sig)
    for c in range(4):
        load(2 + c, rad_hbm.at[pl.ds(c * 8, 8)], rad.at[pl.ds(c * 8, 8)])

    def load_rest():
        load(6, state_hbm, st)
        load(7, lift_hbm, lift)
        load(8, exp_hbm, exp)
        load(9, vol_hbm, vol)
        load(10, target_hbm, target)
        load(11, taper_hbm, taper_ref)
        load(12, wobs_hbm, wobs_ref)
        load(13, wsam_hbm, wsam_ref)
        load(14, host_hbm, host_ref)
        load(15, prof_hbm, prof_ref)

    barrier = pltpu.get_barrier_semaphore()

    def greet(peer):
        pl.semaphore_signal(barrier, inc=1, device_id=peer, device_id_type=MESH)

    for step in steps:
        greet(group_peer(step))
    for dz in range(1, 8):
        greet(z_peer(dz))
    greet((s, a_next))
    greet((s, a_prev))

    @pl.when(s > 0)
    def _():
        greet((s - 1, a))

    @pl.when(s < 7)
    def _():
        greet((s + 1, a))

    ends = (15, 0)
    for way in range(2):
        for k in RELAYS[way]:

            @pl.when(xy == ends[1 - way])
            def _():
                greet((s, (1 - z_hi) * 16 + k))

    loads[0].wait()
    loads[1].wait()
    d0[64:128, :] = jnp.zeros((64, 2048), BF)
    d1[0:64, :] = jnp.zeros((64, 2048), BF)
    for b in range(16):
        cols = slice(b * 128, b * 128 + 128)
        blk = dot(ret[b], sig[:, cols], TN).astype(BF)
        d0[0:64, cols] = blk
        d1[64:128, cols] = blk
    extra = jnp.where(s > 0, 1, 0) + jnp.where(s < 7, 1, 0)
    for k in RELAYS[0] + RELAYS[1]:
        extra = extra + jnp.where(xy == k, 1, 0)

    def send_partial(q, peer):
        pltpu.make_async_remote_copy(
            src_ref=part.at[q], dst_ref=recv_a.at[q_me], send_sem=sa, recv_sem=ra,
            device_id=peer, device_id_type=MESH,
        ).start()

    for g in range(4):
        q0 = g * 8
        loads[2 + g].wait()
        acc = dot(rad[q0 : q0 + 8, 0].reshape(128, 2048), d0[...], NT)
        acc = acc + dot(rad[q0 : q0 + 8, 1].reshape(128, 2048), d1[...], NT)
        part[q0 : q0 + 8] = acc.reshape(8, 16, 128).astype(BF)
        if g == 2:
            load_rest()
        if g == GREETED:
            pl.semaphore_wait(barrier, 40 + extra)
        for t in range(g + 1) if g == GREETED else [g] if g > GREETED else []:
            px = [(t % 2) * 2 + lax.rem(cx + dx, 2) for dx in range(2)]
            for dx in (1, 0):
                for dy in (2, 1, 3, 0):
                    q = px[dx] * 4 + ys[dy]
                    peer = (own_z + t // 2, own_half + q)
                    q = q + (t // 2) * 16
                    if dy != 0:
                        send_partial(q, peer)
                    else:

                        @pl.when(q != q_me)
                        def _():
                            send_partial(q, peer)

    @pl.when(s < 7)
    def _():
        for v in range(5):
            pltpu.make_async_remote_copy(
                src_ref=state_hbm.at[pl.ds(v * 64 + 48, 16), pl.ds(24, 8)],
                dst_ref=ax_recv.at[0, pl.ds(v * 16, 16)],
                send_sem=hx_s.at[0], recv_sem=hx_r.at[0],
                device_id=(s + 1, a), device_id_type=MESH).start()

    @pl.when(s > 0)
    def _():
        for v in range(5):
            pltpu.make_async_remote_copy(
                src_ref=state_hbm.at[pl.ds(v * 64, 16), pl.ds(0, 8)],
                dst_ref=ax_recv.at[1, pl.ds(v * 16, 16)],
                send_sem=hx_s.at[1], recv_sem=hx_r.at[1],
                device_id=(s - 1, a), device_id_type=MESH).start()

    recv_a[q_me] = part[q_me]

    loads[6].wait()

    @pl.loop(0, 40)
    def _(i):
        for j in range(8):
            c = i * 8 + j
            sf[pl.ds(c * PITCH, ROWS), :] = st[c].astype(F32)

    @pl.loop(0, 4)
    def _(x):
        for rhi in range(2):
            col = pl.multiple_of(x * 256 + rhi * 128, 128)
            last = sf[pl.ds(x * 8 + rhi * 4 + 3, 320, stride=PITCH), :].reshape(10, 2, 2, 8, 128)
            packed = jnp.concatenate([last[:, 0, 1, 4:8], last[:, 1, 1, 4:8]], axis=1)
            az_send[0, :, pl.ds(col, 128)] = packed.reshape(80, 128).astype(BF)
            head = sf[pl.ds(x * 8 + rhi * 4, 320, stride=PITCH), :].reshape(10, 2, 2, 8, 128)
            packed = jnp.concatenate([head[:, 0, 0, 0:4], head[:, 1, 0, 0:4]], axis=1)
            az_send[1, :, pl.ds(col, 128)] = packed.reshape(80, 128).astype(BF)

    def az_copy(way, dst):
        return pltpu.make_async_remote_copy(
            src_ref=az_send.at[way], dst_ref=az_recv.at[way], send_sem=ha_s.at[way],
            recv_sem=ha_r.at[way], device_id=(s, dst), device_id_type=MESH)

    az_up, az_dn = az_copy(0, a_next), az_copy(1, a_prev)
    for way, dst in ((0, a_next), (1, a_prev)):

        @pl.when(xy == ends[way])
        def _():
            for i, k in enumerate(RELAYS[way]):
                pltpu.make_async_remote_copy(
                    src_ref=az_send.at[way, pl.ds(16 * i + 16, 16)], dst_ref=relay,
                    send_sem=ha_s.at[way], recv_sem=rel_r,
                    device_id=(s, z_hi * 16 + k), device_id_type=MESH).start()
            piece = pl.ds(0, 16)
            pltpu.make_async_remote_copy(
                src_ref=az_send.at[way, piece], dst_ref=az_recv.at[way, piece],
                send_sem=ha_s.at[way], recv_sem=ha_r.at[way],
                device_id=(s, dst), device_id_type=MESH).start()

    lane = lax.broadcasted_iota(jnp.int32, (80, 128), 1)

    @pl.loop(0, 4)
    def _(x):
        for ay in range(4):
            roll_up, roll_dn = [], []
            for rhi in range(2):
                r = x * 8 + rhi * 4 + ay
                col = pl.multiple_of(x * 256 + rhi * 128, 128)
                f = sf[pl.ds(r, 320, stride=PITCH), :]
                xb = f.astype(BF)
                rhs[ay, 640:960, pl.ds(col, 128)] = xb
                x5 = xb.reshape(5, 64, 128)

                @pl.when(x < 3)
                def _():
                    rhs[ay, 0:80, pl.ds(col + 256, 128)] = x5[:, 48:64].reshape(80, 128)

                @pl.when(x > 0)
                def _():
                    rhs[ay, 80:160, pl.ds(col - 256, 128)] = x5[:, 0:16].reshape(80, 128)

                tiles = f.reshape(20, 2, 8, 128)
                upper = tiles[:, 1]
                lower = tiles[:, 0]
                if ay < 3:
                    rhs[ay + 1, 160:320, pl.ds(col, 128)] = upper.reshape(160, 128).astype(BF)
                if ay > 0:
                    rhs[ay - 1, 320:480, pl.ds(col, 128)] = lower.reshape(160, 128).astype(BF)
                roll_up.append(pltpu.roll(sf[pl.ds(3 * PITCH + r, 80, stride=4 * PITCH), :], 1, 1))
                roll_dn.append(pltpu.roll(sf[pl.ds(r, 80, stride=4 * PITCH), :], 127, 1))
            col = pl.multiple_of(x * 256, 256)
            zero = jnp.zeros((80, 128), F32)
            rhs[ay, 480:560, pl.ds(col, 128)] = jnp.where(lane == 0, zero, roll_up[0]).astype(BF)
            rhs[ay, 480:560, pl.ds(col + 128, 128)] = jnp.where(lane == 0, roll_up[0], roll_up[1]).astype(BF)
            rhs[ay, 560:640, pl.ds(col, 128)] = jnp.where(lane == 127, roll_dn[1], roll_dn[0]).astype(BF)
            rhs[ay, 560:640, pl.ds(col + 128, 128)] = jnp.where(lane == 127, zero, roll_dn[1]).astype(BF)

    @pl.when(xy < 15)
    def _():
        az_up.start()

    @pl.when(xy > 0)
    def _():
        az_dn.start()

    @pl.when(s == 0)
    def _():
        rhs[:, 0:80, 0:256] = jnp.zeros((4, 80, 256), BF)

    @pl.when(s == 7)
    def _():
        rhs[:, 80:160, 768:1024] = jnp.zeros((4, 80, 256), BF)

    for i in (10, 11, 12, 13, 14, 15):
        loads[i].wait()
    for c0, c1 in ((0, 128), (128, 256), (256, 320)):
        line = prof_ref[c0:c1].reshape(1, c1 - c0)
        prof_rows[c0:c1, :] = jnp.transpose(jnp.broadcast_to(line, (128, c1 - c0)))
    kb = pl.multiple_of((q_me // 4) * 128, 128)
    row = pl.multiple_of((q_me % 4) * 32, 32)

    def packed_columns(block):
        tcol[...] = jnp.transpose(block)
        return jnp.concatenate(
            [tcol[pl.ds(row, 16), :], tcol[pl.ds(pl.multiple_of(row + 16, 16), 16), :]], axis=1)

    target_own = packed_columns(target[:, pl.ds(kb, 128)])
    weight_own = packed_columns(taper_ref[...] * wobs_ref[:, pl.ds(kb, 128)])

    pltpu.make_async_copy(part.at[pl.ds(0, 31)], recv_a.at[pl.ds(0, 31)], ra).wait()
    send_b[...] = jnp.sum(recv_a[...].astype(F32), axis=0).astype(BF)
    for dz in (4, 3, 5, 2, 6, 1, 7):
        pltpu.make_async_remote_copy(
            src_ref=send_b, dst_ref=recv_b.at[z_me], send_sem=sb, recv_sem=rb,
            device_id=z_peer(dz), device_id_type=MESH,
        ).start()
    recv_b[z_me] = send_b[...]

    def forward(way):
        for i, k in enumerate(RELAYS[way]):

            @pl.when(xy == k)
            def _():
                pltpu.make_async_copy(az_send.at[0, pl.ds(0, 16)], relay, rel_r).wait()
                rows = pl.ds(16 * i + 16, 16)
                pltpu.make_async_remote_copy(
                    src_ref=relay, dst_ref=az_recv.at[way, rows], send_sem=rel_s, recv_sem=ha_r.at[way],
                    device_id=(s, (1 - z_hi) * 16 + ends[1 - way]), device_id_type=MESH).start()

    forward(0)
    forward(1)

    for i in (7, 8, 9):
        loads[i].wait()
    lf[:, 0:640] = dot(lift[...], exp[...]).astype(BF)
    lf[:, 640:960] = vol[...]

    def sector_row(ay):
        res = dot(lf[...], rhs[ay])
        for x in range(4):
            for rhi in range(2):
                at = (pl.ds(x * 8 + rhi * 4 + ay, 320, stride=PITCH), slice(None))
                col = x * 256 + rhi * 128
                sf[at] = sf[at] + res[:, col : col + 128]

    def axial_halo(side, row, col):
        pltpu.make_async_copy(az_send.at[0], az_recv.at[0], hx_r.at[side]).wait()
        for c in range(80):
            axf[c * FACE_PITCH : c * FACE_PITCH + 8, :] = ax_recv[side, c].astype(F32)
        for rhi in range(2):
            for ay in range(4):
                face = axf[pl.ds(rhi * 4 + ay, 80, stride=FACE_PITCH), :].astype(BF)
                rhs[ay, row : row + 80, col + rhi * 128 : col + rhi * 128 + 128] = face

    @pl.when(s > 0)
    def _():
        axial_halo(0, 0, 0)

    @pl.when(s < 7)
    def _():
        axial_halo(1, 80, 768)

    @pl.loop(1, 3)
    def _(ay):
        sector_row(ay)

    pltpu.make_async_copy(part.at[pl.ds(0, 7)], recv_b.at[pl.ds(0, 7)], rb).wait()
    total = jnp.sum(recv_b[...].astype(F32), axis=0)
    own = weight_own * (total - target_own)
    own_f[...] = own
    sens[q_me] = own.astype(BF)
    for step in steps:
        pltpu.make_async_remote_copy(
            src_ref=sens.at[q_me], dst_ref=sens.at[q_me], send_sem=sc,
            recv_sem=rc.at[0 if step[0] in (0, 3) else 1],
            device_id=group_peer(step), device_id_type=MESH,
        ).start()
    swap = pltpu.make_async_remote_copy(
        src_ref=own_f, dst_ref=other_f, send_sem=sp, recv_sem=rp,
        device_id=((s + 1) - 2 * core, a), device_id_type=MESH)
    swap.start()

    w_hi, w_lo = halves(wsam_ref[...])
    w_lo2 = (wsam_ref[...] - w_hi.astype(F32) - w_lo.astype(F32)).astype(BF)
    w3 = jnp.concatenate([w_hi, w_lo, w_lo2], axis=0)
    g_rows = [jnp.sum(dot(w3, ret[b]), axis=0, keepdims=True) for b in range(16)]
    g_hi, g_lo = halves(jnp.concatenate(g_rows, axis=0))
    gg = jnp.concatenate([g_hi, g_lo], axis=0)
    blank = jnp.zeros((32, 64), BF)
    g0[...] = jnp.concatenate([gg, blank], axis=1)
    g1[...] = jnp.concatenate([blank, gg], axis=1)
    host = host_ref[...]
    lo = host % 128
    oh_lo[...] = jnp.where(lax.broadcasted_iota(jnp.int32, (128, 2048), 0) == lo, 1.0, 0.0).astype(BF)
    hi = host // 128
    point_row = (hi // 8) * 8 + (hi % 2) * 4 + (hi // 2) % 4

    az_up.wait()
    az_dn.wait()
    for x in range(4):
        for rhi in range(2):
            src = slice(x * 256 + rhi * 128, x * 256 + rhi * 128 + 128)
            up = az_recv[0, :, src].astype(F32).reshape(10, 8, 128)
            even = jnp.concatenate([up[:, 4:8], up[:, 0:4]], axis=1)
            both = jnp.concatenate([even[:, None], up[:, None]], axis=1)
            rhs[0, 160:320, src] = both.reshape(160, 128).astype(BF)
            dn = az_recv[1, :, src].astype(F32).reshape(10, 8, 128)
            odd = jnp.concatenate([dn[:, 4:8], dn[:, 0:4]], axis=1)
            both = jnp.concatenate([dn[:, None], odd[:, None]], axis=1)
            rhs[3, 320:480, src] = both.reshape(160, 128).astype(BF)

    @pl.loop(0, 2)
    def _(i):
        sector_row(i * 3)

    def strengths(group):
        blocks = [c * 16 + xs[2 * group + d] * 4 for d in range(2) for c in range(2)]
        flat = jnp.concatenate([sens[pl.ds(q, 4)].reshape(64, 128) for q in blocks], axis=0)
        low = []
        for g in (g0, g1):
            h = dot(g[...], flat, NT)
            low.append(jnp.concatenate(halves(h[0:16] + h[16:32]), axis=0))
        for n in range(4):
            cols = slice(n * 512, n * 512 + 512)
            val = 0.0
            for half in range(2):
                weights = [rad[pl.ds(q, 4), half, :, cols].reshape(64, 512) for q in blocks]
                val = val + dot(low[half], jnp.concatenate(weights, axis=0))
            yield cols, val

    pltpu.make_async_copy(sens.at[pl.ds(0, 15)], sens.at[pl.ds(0, 15)], rc.at[0]).wait()
    for cols, val in strengths(0):
        first[:, cols] = val
    pltpu.make_async_copy(sens.at[pl.ds(0, 16)], sens.at[pl.ds(0, 16)], rc.at[1]).wait()
    block_of = lax.broadcasted_iota(jnp.int32, (32, 512), 0) % 16
    rows = lax.broadcasted_iota(jnp.int32, (32, 512), 0)
    es = jnp.zeros((64, 128), F32)
    for n, (cols, val) in enumerate(strengths(1)):
        mine = lax.broadcasted_iota(jnp.int32, (32, 512), 1) // 128 + n * 4 == block_of
        strength = jnp.sum(jnp.where(mine, first[:, cols] + val, 0.0), axis=0, keepdims=True)
        spread_rows = jnp.where(rows == point_row[:, cols], strength, 0.0)
        pieces = jnp.concatenate(halves(spread_rows), axis=0)
        es = es + dot(pieces, oh_lo[:, cols], NT)
    es_ref[...] = es[0:32] + es[32:64]

    swap.wait()
    mine_f = jnp.where(core == z_hi, own_f[...], other_f[...])
    obs_ref[0:16, :] = mine_f[:, 0:64]
    obs_ref[16:32, :] = mine_f[:, 64:128]

    pltpu.make_async_copy(part.at[pl.ds(0, 31)], recv_a.at[pl.ds(0, 31)], sa).wait()
    pltpu.make_async_copy(part.at[pl.ds(0, 7)], recv_b.at[pl.ds(0, 7)], sb).wait()
    pltpu.make_async_copy(sens.at[pl.ds(0, 31)], sens.at[pl.ds(0, 31)], sc).wait()

    @pl.when(s < 7)
    def _():
        pltpu.make_async_copy(az_send.at[0], az_recv.at[0], hx_s.at[0]).wait()

    @pl.when(s > 0)
    def _():
        pltpu.make_async_copy(az_send.at[0], az_recv.at[0], hx_s.at[1]).wait()

    for k in RELAYS[0] + RELAYS[1]:

        @pl.when(xy == k)
        def _():
            pltpu.make_async_copy(az_send.at[0, pl.ds(0, 16)], relay, rel_s).wait()


def finish(base_ref, es_ref, prof_ref, obs_in, out_hbm, obs_out, buf, sems):
    copies = [pltpu.make_async_copy(obs_in, obs_out, sems.at[FINISH])]
    copies[0].start()
    es = es_ref[...]
    for k in range(FINISH):
        n = 320 // FINISH

        @pl.loop(0, n // 8)
        def _(i):
            for j in range(8):
                c = k * n + i * 8 + j
                rows = pl.ds(pl.multiple_of(c * ROWS, ROWS), ROWS)
                buf[rows, :] = base_ref[pl.ds(c * PITCH, ROWS), :] + prof_ref[pl.ds(c, 1), :] * es

        part = pl.ds(k * n * ROWS, n * ROWS)
        copies.append(pltpu.make_async_copy(buf.at[part], out_hbm.at[part], sems.at[k]))
        copies[-1].start()
    for c in copies:
        c.wait()


def hann_taper(count):
    samples = np.arange(count, dtype=np.float32)
    return (0.5 - 0.5 * np.cos(2.0 * np.pi * (samples + 0.5) / count)).astype(np.float32)


def body(
    surface_signal, retarded_weights, radiation_weights, target_signal, observer_weights,
    sample_weights, host_element, source_profile, adjoint_state, volume_operator, lift_operator,
):
    dma = pltpu.SemaphoreType.DMA
    state = adjoint_state.reshape(320, 4, 4, 2, 128).transpose(0, 1, 3, 2, 4).reshape(320, 32, 128)
    taper = jnp.asarray(np.repeat(hann_taper(64)[:, None], 128, axis=1))
    expand = jnp.asarray(expander(), dtype=BF)
    base, obs_t, es, prof_rows = pl.pallas_call(
        kernel,
        out_shape=(
            pltpu.VMEM((320 * PITCH, 128), F32),
            jax.ShapeDtypeStruct((32, 64), F32),
            jax.ShapeDtypeStruct((32, 128), F32),
            pltpu.VMEM((320, 128), F32),
        ),
        in_specs=[ANY] * 13,
        out_specs=(VM, VM, VM, VM),
        scratch_shapes=[
            pltpu.VMEM((64, 2048), BF),
            pltpu.VMEM((16, 64, 64), BF),
            pltpu.VMEM((32, 2, 16, 2048), BF),
            pltpu.VMEM((320, 32, 128), BF),
            pltpu.VMEM((320, 480), BF),
            pltpu.VMEM((320, 320), BF),
            pltpu.VMEM((480, 640), BF),
            pltpu.VMEM((64, 1024), F32),
            pltpu.VMEM((128, 2048), BF),
            pltpu.VMEM((128, 2048), BF),
            pltpu.VMEM((32, 128), BF),
            pltpu.VMEM((32, 128), BF),
            pltpu.VMEM((32, 16, 128), BF),
            pltpu.VMEM((32, 16, 128), BF),
            pltpu.VMEM((16, 128), BF),
            pltpu.VMEM((8, 16, 128), BF),
            pltpu.VMEM((32, 16, 128), BF),
            pltpu.VMEM((16, 128), F32),
            pltpu.VMEM((16, 128), F32),
            pltpu.VMEM((4, 960, 1024), BF),
            pltpu.VMEM((320, 960), BF),
            pltpu.VMEM((2, 80, 1024), BF),
            pltpu.VMEM((2, 80, 1024), BF),
            pltpu.VMEM((2, 80, 8, 128), BF),
            pltpu.VMEM((80 * FACE_PITCH, 128), F32),
            pltpu.VMEM((128, 2048), BF),
            pltpu.VMEM((128, 64), F32),
            pltpu.VMEM((64, 128), F32),
            pltpu.VMEM((1, 1024), F32),
            pltpu.VMEM((1, 64), F32),
            pltpu.VMEM((1, 2048), jnp.int32),
            pltpu.VMEM((320,), F32),
            pltpu.VMEM((16, 1024), BF),
            pltpu.VMEM((32, 2048), F32),
            dma((16,)),
            dma, dma, dma, dma, dma, dma((2,)), dma, dma,
            dma((2,)), dma((2,)), dma((2,)), dma((2,)), dma, dma,
        ],
        compiler_params=pltpu.CompilerParams(
            collective_id=0, has_side_effects=True, vmem_limit_bytes=48 * 1024 * 1024
        ),
    )(
        *(
            pltpu.with_memory_space_constraint(x, pltpu.HBM)
            for x in (
                surface_signal,
                retarded_weights,
                radiation_weights.reshape(32, 2, 16, 2048),
                state,
                lift_operator,
                volume_operator,
                expand,
                target_signal,
                taper,
                observer_weights.reshape(1, 1024),
                sample_weights.reshape(1, 64),
                host_element.reshape(1, 2048),
                source_profile,
            )
        )
    )
    updated, obs_t = pl.pallas_call(
        finish,
        out_shape=(
            jax.ShapeDtypeStruct((10240, 128), F32),
            jax.ShapeDtypeStruct((32, 64), F32),
        ),
        in_specs=[VM, VM, VM, VM],
        out_specs=(ANY, ANY),
        scratch_shapes=[pltpu.VMEM((10240, 128), F32), dma((FINISH + 1,))],
        compiler_params=pltpu.CompilerParams(vmem_limit_bytes=16 * 1024 * 1024),
    )(
        pltpu.with_memory_space_constraint(base, pltpu.VMEM),
        es,
        pltpu.with_memory_space_constraint(prof_rows, pltpu.VMEM),
        obs_t,
    )
    updated = updated.reshape(320, 4, 2, 4, 128).transpose(0, 1, 3, 2, 4)
    return (obs_t.T, updated.reshape(320, 4, 4, 256))


def solution(mesh):
    return jax.shard_map(
        body,
        mesh=mesh,
        in_specs=(
            P(None, ("stream", "azim")),
            P(("stream", "azim"), None, None),
            P(None, ("stream", "azim")),
            P(),
            P(),
            P(),
            P(("stream", "azim")),
            P(),
            P(None, "stream", "azim", None),
            P(),
            P(),
        ),
        out_specs=(P(None, "azim"), P(None, "stream", "azim", None)),
        check_vma=False,
    )
```

```python
import jax
import jax.numpy as jnp
import numpy as np
from jax import lax
from jax.experimental import pallas as pl
from jax.experimental.pallas import tpu as pltpu
from jax.sharding import PartitionSpec as P

MESH = pl.DeviceIdType.MESH
BF = jnp.bfloat16
F32 = jnp.float32
ANY = pl.BlockSpec(memory_space=pl.ANY)
VM = pl.BlockSpec(memory_space=pltpu.VMEM)
FINISH = 10
GREETED = 2
ROWS = 32
PITCH = 33
FACE_PITCH = 9
RELAYS = ((12, 3, 14, 11), (1, 4, 13, 7))
NT = (((1,), (1,)), ((), ()))
TN = (((0,), (0,)), ((), ()))


def dot(a, b, dims=(((1,), (0,)), ((), ()))):
    return lax.dot_general(a, b, dims, preferred_element_type=F32)


def halves(x):
    top = x.astype(BF)
    return top, (x - top.astype(F32)).astype(BF)


def peers_by_distance():
    def hops(d):
        return min(d, 4 - d)

    steps = [(dx, dy, dc) for dx in range(4) for dy in range(4) for dc in range(2)]
    steps = [s for s in steps if s != (0, 0, 0)]
    return sorted(steps, key=lambda s: -(hops(s[0]) + hops(s[1])))


def expander():
    e = np.zeros((480, 640), np.float32)
    for j in range(160):
        e[j, j] = 1.0
    for vp in range(20):
        for w in range(4):
            e[160 + vp * 4 + w, 160 + vp * 8 + 4 + w] = 1.0
            e[240 + vp * 4 + w, 320 + vp * 8 + w] = 1.0
    for j in range(160):
        e[320 + j, 480 + j] = 1.0
    return e


def kernel(
    sig_hbm, ret_hbm, rad_hbm, state_hbm, lift_hbm, vol_hbm, exp_hbm, target_hbm,
    taper_hbm, wobs_hbm, wsam_hbm, host_hbm, prof_hbm,
    sf, obs_ref, es_ref, prof_rows,
    sig, ret, rad, st, lift, vol, exp, target,
    d0, d1, g0, g1, part, recv_a, send_b, recv_b, sens, own_f, other_f,
    rhs, lf, az_send, az_recv, ax_recv, axf, oh_lo, tcol,
    taper_ref, wobs_ref, wsam_ref, host_ref, prof_ref, relay, first,
    ld, sa, ra, sb, rb, sc, rc, sp, rp, hx_s, hx_r, ha_s, ha_r, rel_s, rel_r,
):
    s = lax.axis_index("stream")
    a = lax.axis_index("azim")
    z_lo = s // 2
    core = s - z_lo * 2
    z_hi = a // 16
    xy = a - z_hi * 16
    cx = xy // 4
    cy = xy - cx * 4
    q_me = core * 16 + xy
    z_me = z_hi * 4 + z_lo
    steps = peers_by_distance()

    xs = [lax.rem(cx + d, 4) for d in range(4)]
    ys = [lax.rem(cy + d, 4) for d in range(4)]
    cs = [core, 1 - core]
    zs = [lax.rem(z_me + d, 8) for d in range(8)]
    own_z, own_half = z_lo * 2, z_hi * 16

    def group_peer(step):
        dx, dy, dc = step
        return own_z + cs[dc], own_half + xs[dx] * 4 + ys[dy]

    def z_peer(dz):
        half = zs[dz] // 4
        return (zs[dz] - half * 4) * 2 + core, half * 16 + xy

    a_next, a_prev = lax.rem(a + 1, 32), lax.rem(a + 31, 32)

    loads = {}

    def load(i, src, dst):
        loads[i] = pltpu.make_async_copy(src, dst, ld.at[i])
        loads[i].start()

    load(0, ret_hbm, ret)
    load(1, sig_hbm, sig)
    for c in range(4):
        load(2 + c, rad_hbm.at[pl.ds(c * 8, 8)], rad.at[pl.ds(c * 8, 8)])

    def load_rest():
        load(6, state_hbm, st)
        load(7, lift_hbm, lift)
        load(8, exp_hbm, exp)
        load(9, vol_hbm, vol)
        load(10, target_hbm, target)
        load(11, taper_hbm, taper_ref)
        load(12, wobs_hbm, wobs_ref)
        load(13, wsam_hbm, wsam_ref)
        load(14, host_hbm, host_ref)
        load(15, prof_hbm, prof_ref)

    barrier = pltpu.get_barrier_semaphore()

    def greet(peer):
        pl.semaphore_signal(barrier, inc=1, device_id=peer, device_id_type=MESH)

    ends = (15, 0)
    for way in range(2):

        @pl.when(xy == ends[1 - way])
        def _():
            for k in RELAYS[way]:
                greet((s, (1 - z_hi) * 16 + k))

    greet(z_peer(4))
    for step in steps[:2]:
        greet(group_peer(step))
    greet((s, a_next))
    greet((s, a_prev))
    for dz in (3, 5):
        greet(z_peer(dz))

    @pl.when(s > 0)
    def _():
        greet((s - 1, a))

    @pl.when(s < 7)
    def _():
        greet((s + 1, a))

    for step in steps[2:]:
        greet(group_peer(step))
    for dz in (2, 6, 1, 7):
        greet(z_peer(dz))

    loads[0].wait()
    loads[1].wait()
    d0[64:128, :] = jnp.zeros((64, 2048), BF)
    d1[0:64, :] = jnp.zeros((64, 2048), BF)
    for b in range(16):
        cols = slice(b * 128, b * 128 + 128)
        blk = dot(ret[b], sig[:, cols], TN).astype(BF)
        d0[0:64, cols] = blk
        d1[64:128, cols] = blk
    extra = jnp.where(s > 0, 1, 0) + jnp.where(s < 7, 1, 0)
    for k in RELAYS[0] + RELAYS[1]:
        extra = extra + jnp.where(xy == k, 1, 0)

    def send_partial(q, peer):
        pltpu.make_async_remote_copy(
            src_ref=part.at[q], dst_ref=recv_a.at[q_me], send_sem=sa, recv_sem=ra,
            device_id=peer, device_id_type=MESH,
        ).start()

    for g in range(4):
        q0 = g * 8
        loads[2 + g].wait()
        acc = dot(rad[q0 : q0 + 8, 0].reshape(128, 2048), d0[...], NT)
        acc = acc + dot(rad[q0 : q0 + 8, 1].reshape(128, 2048), d1[...], NT)
        part[q0 : q0 + 8] = acc.reshape(8, 16, 128).astype(BF)
        if g == 2:
            load_rest()
        if g == GREETED:
            pl.semaphore_wait(barrier, 40 + extra)
        for t in range(g + 1) if g == GREETED else [g] if g > GREETED else []:
            px = [(t % 2) * 2 + lax.rem(cx + dx, 2) for dx in range(2)]
            for dx in (1, 0):
                for dy in (2, 1, 3, 0):
                    q = px[dx] * 4 + ys[dy]
                    peer = (own_z + t // 2, own_half + q)
                    q = q + (t // 2) * 16
                    if dy != 0:
                        send_partial(q, peer)
                    else:

                        @pl.when(q != q_me)
                        def _():
                            send_partial(q, peer)

    @pl.when(s < 7)
    def _():
        for v in range(5):
            pltpu.make_async_remote_copy(
                src_ref=state_hbm.at[pl.ds(v * 64 + 48, 16), pl.ds(24, 8)],
                dst_ref=ax_recv.at[0, pl.ds(v * 16, 16)],
                send_sem=hx_s.at[0], recv_sem=hx_r.at[0],
                device_id=(s + 1, a), device_id_type=MESH).start()

    @pl.when(s > 0)
    def _():
        for v in range(5):
            pltpu.make_async_remote_copy(
                src_ref=state_hbm.at[pl.ds(v * 64, 16), pl.ds(0, 8)],
                dst_ref=ax_recv.at[1, pl.ds(v * 16, 16)],
                send_sem=hx_s.at[1], recv_sem=hx_r.at[1],
                device_id=(s - 1, a), device_id_type=MESH).start()

    recv_a[q_me] = part[q_me]

    loads[6].wait()

    @pl.loop(0, 40)
    def _(i):
        for j in range(8):
            c = i * 8 + j
            sf[pl.ds(c * PITCH, ROWS), :] = st[c].astype(F32)

    @pl.loop(0, 4)
    def _(x):
        for rhi in range(2):
            col = pl.multiple_of(x * 256 + rhi * 128, 128)
            last = sf[pl.ds(x * 8 + rhi * 4 + 3, 320, stride=PITCH), :].reshape(10, 2, 2, 8, 128)
            packed = jnp.concatenate([last[:, 0, 1, 4:8], last[:, 1, 1, 4:8]], axis=1)
            az_send[0, :, pl.ds(col, 128)] = packed.reshape(80, 128).astype(BF)
            head = sf[pl.ds(x * 8 + rhi * 4, 320, stride=PITCH), :].reshape(10, 2, 2, 8, 128)
            packed = jnp.concatenate([head[:, 0, 0, 0:4], head[:, 1, 0, 0:4]], axis=1)
            az_send[1, :, pl.ds(col, 128)] = packed.reshape(80, 128).astype(BF)

    def az_copy(way, dst):
        return pltpu.make_async_remote_copy(
            src_ref=az_send.at[way], dst_ref=az_recv.at[way], send_sem=ha_s.at[way],
            recv_sem=ha_r.at[way], device_id=(s, dst), device_id_type=MESH)

    az_up, az_dn = az_copy(0, a_next), az_copy(1, a_prev)
    for way, dst in ((0, a_next), (1, a_prev)):

        @pl.when(xy == ends[way])
        def _():
            for i, k in enumerate(RELAYS[way]):
                pltpu.make_async_remote_copy(
                    src_ref=az_send.at[way, pl.ds(16 * i + 16, 16)], dst_ref=relay,
                    send_sem=ha_s.at[way], recv_sem=rel_r,
                    device_id=(s, z_hi * 16 + k), device_id_type=MESH).start()
            piece = pl.ds(0, 16)
            pltpu.make_async_remote_copy(
                src_ref=az_send.at[way, piece], dst_ref=az_recv.at[way, piece],
                send_sem=ha_s.at[way], recv_sem=ha_r.at[way],
                device_id=(s, dst), device_id_type=MESH).start()

    lane = lax.broadcasted_iota(jnp.int32, (80, 128), 1)

    @pl.loop(0, 4)
    def _(x):
        for ay in range(4):
            roll_up, roll_dn = [], []
            for rhi in range(2):
                r = x * 8 + rhi * 4 + ay
                col = pl.multiple_of(x * 256 + rhi * 128, 128)
                f = sf[pl.ds(r, 320, stride=PITCH), :]
                xb = f.astype(BF)
                rhs[ay, 640:960, pl.ds(col, 128)] = xb
                x5 = xb.reshape(5, 64, 128)

                @pl.when(x < 3)
                def _():
                    rhs[ay, 0:80, pl.ds(col + 256, 128)] = x5[:, 48:64].reshape(80, 128)

                @pl.when(x > 0)
                def _():
                    rhs[ay, 80:160, pl.ds(col - 256, 128)] = x5[:, 0:16].reshape(80, 128)

                tiles = f.reshape(20, 2, 8, 128)
                upper = tiles[:, 1]
                lower = tiles[:, 0]
                if ay < 3:
                    rhs[ay + 1, 160:320, pl.ds(col, 128)] = upper.reshape(160, 128).astype(BF)
                if ay > 0:
                    rhs[ay - 1, 320:480, pl.ds(col, 128)] = lower.reshape(160, 128).astype(BF)
                roll_up.append(pltpu.roll(sf[pl.ds(3 * PITCH + r, 80, stride=4 * PITCH), :], 1, 1))
                roll_dn.append(pltpu.roll(sf[pl.ds(r, 80, stride=4 * PITCH), :], 127, 1))
            col = pl.multiple_of(x * 256, 256)
            zero = jnp.zeros((80, 128), F32)
            rhs[ay, 480:560, pl.ds(col, 128)] = jnp.where(lane == 0, zero, roll_up[0]).astype(BF)
            rhs[ay, 480:560, pl.ds(col + 128, 128)] = jnp.where(lane == 0, roll_up[0], roll_up[1]).astype(BF)
            rhs[ay, 560:640, pl.ds(col, 128)] = jnp.where(lane == 127, roll_dn[1], roll_dn[0]).astype(BF)
            rhs[ay, 560:640, pl.ds(col + 128, 128)] = jnp.where(lane == 127, zero, roll_dn[1]).astype(BF)

    @pl.when(xy < 15)
    def _():
        az_up.start()

    @pl.when(xy > 0)
    def _():
        az_dn.start()

    @pl.when(s == 0)
    def _():
        rhs[:, 0:80, 0:256] = jnp.zeros((4, 80, 256), BF)

    @pl.when(s == 7)
    def _():
        rhs[:, 80:160, 768:1024] = jnp.zeros((4, 80, 256), BF)

    for i in (10, 11, 12, 13, 14, 15):
        loads[i].wait()
    for c0, c1 in ((0, 128), (128, 256), (256, 320)):
        line = prof_ref[c0:c1].reshape(1, c1 - c0)
        prof_rows[c0:c1, :] = jnp.transpose(jnp.broadcast_to(line, (128, c1 - c0)))
    kb = pl.multiple_of((q_me // 4) * 128, 128)
    row = pl.multiple_of((q_me % 4) * 32, 32)

    def packed_columns(block):
        tcol[...] = jnp.transpose(block)
        return jnp.concatenate(
            [tcol[pl.ds(row, 16), :], tcol[pl.ds(pl.multiple_of(row + 16, 16), 16), :]], axis=1)

    target_own = packed_columns(target[:, pl.ds(kb, 128)])
    weight_own = packed_columns(taper_ref[...] * wobs_ref[:, pl.ds(kb, 128)])

    pltpu.make_async_copy(part.at[pl.ds(0, 31)], recv_a.at[pl.ds(0, 31)], ra).wait()
    send_b[...] = jnp.sum(recv_a[...].astype(F32), axis=0).astype(BF)
    for dz in (4, 3, 5, 2, 6, 1, 7):
        pltpu.make_async_remote_copy(
            src_ref=send_b, dst_ref=recv_b.at[z_me], send_sem=sb, recv_sem=rb,
            device_id=z_peer(dz), device_id_type=MESH,
        ).start()
    recv_b[z_me] = send_b[...]

    def forward(way):
        for i, k in enumerate(RELAYS[way]):

            @pl.when(xy == k)
            def _():
                pltpu.make_async_copy(az_send.at[0, pl.ds(0, 16)], relay, rel_r).wait()
                rows = pl.ds(16 * i + 16, 16)
                pltpu.make_async_remote_copy(
                    src_ref=relay, dst_ref=az_recv.at[way, rows], send_sem=rel_s, recv_sem=ha_r.at[way],
                    device_id=(s, (1 - z_hi) * 16 + ends[1 - way]), device_id_type=MESH).start()

    forward(0)
    forward(1)

    for i in (7, 8, 9):
        loads[i].wait()
    lf[:, 0:640] = dot(lift[...], exp[...]).astype(BF)
    lf[:, 640:960] = vol[...]

    def sector_row(ay):
        res = dot(lf[...], rhs[ay])
        for x in range(4):
            for rhi in range(2):
                at = (pl.ds(x * 8 + rhi * 4 + ay, 320, stride=PITCH), slice(None))
                col = x * 256 + rhi * 128
                sf[at] = sf[at] + res[:, col : col + 128]

    def axial_halo(side, row, col):
        pltpu.make_async_copy(az_send.at[0], az_recv.at[0], hx_r.at[side]).wait()
        for c in range(80):
            axf[c * FACE_PITCH : c * FACE_PITCH + 8, :] = ax_recv[side, c].astype(F32)
        for rhi in range(2):
            for ay in range(4):
                face = axf[pl.ds(rhi * 4 + ay, 80, stride=FACE_PITCH), :].astype(BF)
                rhs[ay, row : row + 80, col + rhi * 128 : col + rhi * 128 + 128] = face

    @pl.when(s > 0)
    def _():
        axial_halo(0, 0, 0)

    @pl.when(s < 7)
    def _():
        axial_halo(1, 80, 768)

    @pl.loop(1, 3)
    def _(ay):
        sector_row(ay)

    pltpu.make_async_copy(part.at[pl.ds(0, 7)], recv_b.at[pl.ds(0, 7)], rb).wait()
    total = jnp.sum(recv_b[...].astype(F32), axis=0)
    own = weight_own * (total - target_own)
    own_f[...] = own
    sens[q_me] = own.astype(BF)
    for step in steps:
        pltpu.make_async_remote_copy(
            src_ref=sens.at[q_me], dst_ref=sens.at[q_me], send_sem=sc,
            recv_sem=rc.at[0 if step[0] in (0, 3) else 1],
            device_id=group_peer(step), device_id_type=MESH,
        ).start()
    swap = pltpu.make_async_remote_copy(
        src_ref=own_f, dst_ref=other_f, send_sem=sp, recv_sem=rp,
        device_id=((s + 1) - 2 * core, a), device_id_type=MESH)
    swap.start()

    w_hi, w_lo = halves(wsam_ref[...])
    w_lo2 = (wsam_ref[...] - w_hi.astype(F32) - w_lo.astype(F32)).astype(BF)
    w3 = jnp.concatenate([w_hi, w_lo, w_lo2], axis=0)
    g_rows = [jnp.sum(dot(w3, ret[b]), axis=0, keepdims=True) for b in range(16)]
    g_hi, g_lo = halves(jnp.concatenate(g_rows, axis=0))
    gg = jnp.concatenate([g_hi, g_lo], axis=0)
    blank = jnp.zeros((32, 64), BF)
    g0[...] = jnp.concatenate([gg, blank], axis=1)
    g1[...] = jnp.concatenate([blank, gg], axis=1)
    host = host_ref[...]
    lo = host % 128
    oh_lo[...] = jnp.where(lax.broadcasted_iota(jnp.int32, (128, 2048), 0) == lo, 1.0, 0.0).astype(BF)
    hi = host // 128
    point_row = (hi // 8) * 8 + (hi % 2) * 4 + (hi // 2) % 4

    az_up.wait()
    az_dn.wait()
    for x in range(4):
        for rhi in range(2):
            src = slice(x * 256 + rhi * 128, x * 256 + rhi * 128 + 128)
            up = az_recv[0, :, src].astype(F32).reshape(10, 8, 128)
            even = jnp.concatenate([up[:, 4:8], up[:, 0:4]], axis=1)
            both = jnp.concatenate([even[:, None], up[:, None]], axis=1)
            rhs[0, 160:320, src] = both.reshape(160, 128).astype(BF)
            dn = az_recv[1, :, src].astype(F32).reshape(10, 8, 128)
            odd = jnp.concatenate([dn[:, 4:8], dn[:, 0:4]], axis=1)
            both = jnp.concatenate([dn[:, None], odd[:, None]], axis=1)
            rhs[3, 320:480, src] = both.reshape(160, 128).astype(BF)

    @pl.loop(0, 2)
    def _(i):
        sector_row(i * 3)

    def strengths(group):
        blocks = [c * 16 + xs[2 * group + d] * 4 for d in range(2) for c in range(2)]
        flat = jnp.concatenate([sens[pl.ds(q, 4)].reshape(64, 128) for q in blocks], axis=0)
        low = []
        for g in (g0, g1):
            h = dot(g[...], flat, NT)
            low.append(jnp.concatenate(halves(h[0:16] + h[16:32]), axis=0))
        for n in range(4):
            cols = slice(n * 512, n * 512 + 512)
            val = 0.0
            for half in range(2):
                weights = [rad[pl.ds(q, 4), half, :, cols].reshape(64, 512) for q in blocks]
                val = val + dot(low[half], jnp.concatenate(weights, axis=0))
            yield cols, val

    pltpu.make_async_copy(sens.at[pl.ds(0, 15)], sens.at[pl.ds(0, 15)], rc.at[0]).wait()
    for cols, val in strengths(0):
        first[:, cols] = val
    pltpu.make_async_copy(sens.at[pl.ds(0, 16)], sens.at[pl.ds(0, 16)], rc.at[1]).wait()
    block_of = lax.broadcasted_iota(jnp.int32, (32, 512), 0) % 16
    rows = lax.broadcasted_iota(jnp.int32, (32, 512), 0)
    es = jnp.zeros((64, 128), F32)
    for n, (cols, val) in enumerate(strengths(1)):
        mine = lax.broadcasted_iota(jnp.int32, (32, 512), 1) // 128 + n * 4 == block_of
        strength = jnp.sum(jnp.where(mine, first[:, cols] + val, 0.0), axis=0, keepdims=True)
        spread_rows = jnp.where(rows == point_row[:, cols], strength, 0.0)
        pieces = jnp.concatenate(halves(spread_rows), axis=0)
        es = es + dot(pieces, oh_lo[:, cols], NT)
    es_ref[...] = es[0:32] + es[32:64]

    swap.wait()
    mine_f = jnp.where(core == z_hi, own_f[...], other_f[...])
    obs_ref[0:16, :] = mine_f[:, 0:64]
    obs_ref[16:32, :] = mine_f[:, 64:128]

    pltpu.make_async_copy(part.at[pl.ds(0, 31)], recv_a.at[pl.ds(0, 31)], sa).wait()
    pltpu.make_async_copy(part.at[pl.ds(0, 7)], recv_b.at[pl.ds(0, 7)], sb).wait()
    pltpu.make_async_copy(sens.at[pl.ds(0, 31)], sens.at[pl.ds(0, 31)], sc).wait()

    @pl.when(s < 7)
    def _():
        pltpu.make_async_copy(az_send.at[0], az_recv.at[0], hx_s.at[0]).wait()

    @pl.when(s > 0)
    def _():
        pltpu.make_async_copy(az_send.at[0], az_recv.at[0], hx_s.at[1]).wait()

    for k in RELAYS[0] + RELAYS[1]:

        @pl.when(xy == k)
        def _():
            pltpu.make_async_copy(az_send.at[0, pl.ds(0, 16)], relay, rel_s).wait()


def finish(base_ref, es_ref, prof_ref, obs_in, out_hbm, obs_out, buf, sems):
    copies = [pltpu.make_async_copy(obs_in, obs_out, sems.at[FINISH])]
    copies[0].start()
    es = es_ref[...]
    for k in range(FINISH):
        n = 320 // FINISH

        @pl.loop(0, n // 8)
        def _(i):
            for j in range(8):
                c = k * n + i * 8 + j
                rows = pl.ds(pl.multiple_of(c * ROWS, ROWS), ROWS)
                buf[rows, :] = base_ref[pl.ds(c * PITCH, ROWS), :] + prof_ref[pl.ds(c, 1), :] * es

        part = pl.ds(k * n * ROWS, n * ROWS)
        copies.append(pltpu.make_async_copy(buf.at[part], out_hbm.at[part], sems.at[k]))
        copies[-1].start()
    for c in copies:
        c.wait()


def hann_taper(count):
    samples = np.arange(count, dtype=np.float32)
    return (0.5 - 0.5 * np.cos(2.0 * np.pi * (samples + 0.5) / count)).astype(np.float32)


def body(
    surface_signal, retarded_weights, radiation_weights, target_signal, observer_weights,
    sample_weights, host_element, source_profile, adjoint_state, volume_operator, lift_operator,
):
    dma = pltpu.SemaphoreType.DMA
    state = adjoint_state.reshape(320, 4, 4, 2, 128).transpose(0, 1, 3, 2, 4).reshape(320, 32, 128)
    taper = jnp.asarray(np.repeat(hann_taper(64)[:, None], 128, axis=1))
    expand = jnp.asarray(expander(), dtype=BF)
    base, obs_t, es, prof_rows = pl.pallas_call(
        kernel,
        out_shape=(
            pltpu.VMEM((320 * PITCH, 128), F32),
            jax.ShapeDtypeStruct((32, 64), F32),
            jax.ShapeDtypeStruct((32, 128), F32),
            pltpu.VMEM((320, 128), F32),
        ),
        in_specs=[ANY] * 13,
        out_specs=(VM, VM, VM, VM),
        scratch_shapes=[
            pltpu.VMEM((64, 2048), BF),
            pltpu.VMEM((16, 64, 64), BF),
            pltpu.VMEM((32, 2, 16, 2048), BF),
            pltpu.VMEM((320, 32, 128), BF),
            pltpu.VMEM((320, 480), BF),
            pltpu.VMEM((320, 320), BF),
            pltpu.VMEM((480, 640), BF),
            pltpu.VMEM((64, 1024), F32),
            pltpu.VMEM((128, 2048), BF),
            pltpu.VMEM((128, 2048), BF),
            pltpu.VMEM((32, 128), BF),
            pltpu.VMEM((32, 128), BF),
            pltpu.VMEM((32, 16, 128), BF),
            pltpu.VMEM((32, 16, 128), BF),
            pltpu.VMEM((16, 128), BF),
            pltpu.VMEM((8, 16, 128), BF),
            pltpu.VMEM((32, 16, 128), BF),
            pltpu.VMEM((16, 128), F32),
            pltpu.VMEM((16, 128), F32),
            pltpu.VMEM((4, 960, 1024), BF),
            pltpu.VMEM((320, 960), BF),
            pltpu.VMEM((2, 80, 1024), BF),
            pltpu.VMEM((2, 80, 1024), BF),
            pltpu.VMEM((2, 80, 8, 128), BF),
            pltpu.VMEM((80 * FACE_PITCH, 128), F32),
            pltpu.VMEM((128, 2048), BF),
            pltpu.VMEM((128, 64), F32),
            pltpu.VMEM((64, 128), F32),
            pltpu.VMEM((1, 1024), F32),
            pltpu.VMEM((1, 64), F32),
            pltpu.VMEM((1, 2048), jnp.int32),
            pltpu.VMEM((320,), F32),
            pltpu.VMEM((16, 1024), BF),
            pltpu.VMEM((32, 2048), F32),
            dma((16,)),
            dma, dma, dma, dma, dma, dma((2,)), dma, dma,
            dma((2,)), dma((2,)), dma((2,)), dma((2,)), dma, dma,
        ],
        compiler_params=pltpu.CompilerParams(
            collective_id=0, has_side_effects=True, vmem_limit_bytes=48 * 1024 * 1024
        ),
    )(
        *(
            pltpu.with_memory_space_constraint(x, pltpu.HBM)
            for x in (
                surface_signal,
                retarded_weights,
                radiation_weights.reshape(32, 2, 16, 2048),
                state,
                lift_operator,
                volume_operator,
                expand,
                target_signal,
                taper,
                observer_weights.reshape(1, 1024),
                sample_weights.reshape(1, 64),
                host_element.reshape(1, 2048),
                source_profile,
            )
        )
    )
    updated, obs_t = pl.pallas_call(
        finish,
        out_shape=(
            jax.ShapeDtypeStruct((10240, 128), F32),
            jax.ShapeDtypeStruct((32, 64), F32),
        ),
        in_specs=[VM, VM, VM, VM],
        out_specs=(ANY, ANY),
        scratch_shapes=[pltpu.VMEM((10240, 128), F32), dma((FINISH + 1,))],
        compiler_params=pltpu.CompilerParams(vmem_limit_bytes=16 * 1024 * 1024),
    )(
        pltpu.with_memory_space_constraint(base, pltpu.VMEM),
        es,
        pltpu.with_memory_space_constraint(prof_rows, pltpu.VMEM),
        obs_t,
    )
    updated = updated.reshape(320, 4, 2, 4, 128).transpose(0, 1, 3, 2, 4)
    return (obs_t.T, updated.reshape(320, 4, 4, 256))


def solution(mesh):
    return jax.shard_map(
        body,
        mesh=mesh,
        in_specs=(
            P(None, ("stream", "azim")),
            P(("stream", "azim"), None, None),
            P(None, ("stream", "azim")),
            P(),
            P(),
            P(),
            P(("stream", "azim")),
            P(),
            P(None, "stream", "azim", None),
            P(),
            P(),
        ),
        out_specs=(P(None, "azim"), P(None, "stream", "azim", None)),
        check_vma=False,
    )
```

```python
import jax
import jax.numpy as jnp
import numpy as np
from jax import lax
from jax.experimental import pallas as pl
from jax.experimental.pallas import tpu as pltpu
from jax.sharding import PartitionSpec as P

MESH = pl.DeviceIdType.MESH
BF = jnp.bfloat16
F32 = jnp.float32
ANY = pl.BlockSpec(memory_space=pl.ANY)
VM = pl.BlockSpec(memory_space=pltpu.VMEM)
FINISH = 10
GREETED = 2
ROWS = 32
PITCH = 33
FACE_PITCH = 9
RELAYS = ((12, 3, 14, 11), (1, 4, 13, 7))
NT = (((1,), (1,)), ((), ()))
TN = (((0,), (0,)), ((), ()))


def dot(a, b, dims=(((1,), (0,)), ((), ()))):
    return lax.dot_general(a, b, dims, preferred_element_type=F32)


def halves(x):
    top = x.astype(BF)
    return top, (x - top.astype(F32)).astype(BF)


def peers_by_distance():
    def hops(d):
        return min(d, 4 - d)

    steps = [(dx, dy, dc) for dx in range(4) for dy in range(4) for dc in range(2)]
    steps = [s for s in steps if s != (0, 0, 0)]
    return sorted(steps, key=lambda s: -(hops(s[0]) + hops(s[1])))


def expander():
    e = np.zeros((480, 640), np.float32)
    for j in range(160):
        e[j, j] = 1.0
    for vp in range(20):
        for w in range(4):
            e[160 + vp * 4 + w, 160 + vp * 8 + 4 + w] = 1.0
            e[240 + vp * 4 + w, 320 + vp * 8 + w] = 1.0
    for j in range(160):
        e[320 + j, 480 + j] = 1.0
    return e


def kernel(
    sig_hbm, ret_hbm, rad_hbm, state_hbm, lift_hbm, vol_hbm, exp_hbm, target_hbm,
    taper_hbm, wobs_hbm, wsam_hbm, host_hbm, prof_hbm,
    sf, obs_ref, es_ref, prof_rows,
    sig, ret, rad, st, lift, vol, exp, target,
    d0, d1, g0, g1, part, recv_a, send_b, recv_b, sens, own_f, other_f,
    rhs, lf, az_send, az_recv, ax_recv, axf, oh_lo, tcol,
    taper_ref, wobs_ref, wsam_ref, host_ref, prof_ref, relay, first,
    ld, sa, ra, sb, rb, sc, rc, sp, rp, hx_s, hx_r, ha_s, ha_r, rel_s, rel_r,
):
    s = lax.axis_index("stream")
    a = lax.axis_index("azim")
    z_lo = s // 2
    core = s - z_lo * 2
    z_hi = a // 16
    xy = a - z_hi * 16
    cx = xy // 4
    cy = xy - cx * 4
    q_me = core * 16 + xy
    z_me = z_hi * 4 + z_lo
    steps = peers_by_distance()

    xs = [lax.rem(cx + d, 4) for d in range(4)]
    ys = [lax.rem(cy + d, 4) for d in range(4)]
    cs = [core, 1 - core]
    zs = [lax.rem(z_me + d, 8) for d in range(8)]
    own_z, own_half = z_lo * 2, z_hi * 16

    def group_peer(step):
        dx, dy, dc = step
        return own_z + cs[dc], own_half + xs[dx] * 4 + ys[dy]

    def z_peer(dz):
        half = zs[dz] // 4
        return (zs[dz] - half * 4) * 2 + core, half * 16 + xy

    a_next, a_prev = lax.rem(a + 1, 32), lax.rem(a + 31, 32)

    loads = {}

    def load(i, src, dst):
        loads[i] = pltpu.make_async_copy(src, dst, ld.at[i])
        loads[i].start()

    load(0, ret_hbm, ret)
    load(1, sig_hbm, sig)
    for c in range(4):
        load(2 + c, rad_hbm.at[pl.ds(c * 8, 8)], rad.at[pl.ds(c * 8, 8)])

    def load_rest():
        load(6, state_hbm, st)
        load(7, lift_hbm, lift)
        load(8, exp_hbm, exp)
        load(9, vol_hbm, vol)
        load(10, target_hbm, target)
        load(11, taper_hbm, taper_ref)
        load(12, wobs_hbm, wobs_ref)
        load(13, wsam_hbm, wsam_ref)
        load(14, host_hbm, host_ref)
        load(15, prof_hbm, prof_ref)

    barrier = pltpu.get_barrier_semaphore()

    def greet(peer):
        pl.semaphore_signal(barrier, inc=1, device_id=peer, device_id_type=MESH)

    ends = (15, 0)
    for way in range(2):

        @pl.when(xy == ends[1 - way])
        def _():
            for k in RELAYS[way]:
                greet((s, (1 - z_hi) * 16 + k))

    greet(z_peer(4))
    for step in steps[:2]:
        greet(group_peer(step))
    greet((s, a_next))
    greet((s, a_prev))
    for dz in (3, 5):
        greet(z_peer(dz))

    @pl.when(s > 0)
    def _():
        greet((s - 1, a))

    @pl.when(s < 7)
    def _():
        greet((s + 1, a))

    for step in steps[2:]:
        greet(group_peer(step))
    for dz in (2, 6, 1, 7):
        greet(z_peer(dz))

    loads[0].wait()
    loads[1].wait()
    d0[64:128, :] = jnp.zeros((64, 2048), BF)
    d1[0:64, :] = jnp.zeros((64, 2048), BF)
    for b in range(16):
        cols = slice(b * 128, b * 128 + 128)
        blk = dot(ret[b], sig[:, cols], TN).astype(BF)
        d0[0:64, cols] = blk
        d1[64:128, cols] = blk
    extra = jnp.where(s > 0, 1, 0) + jnp.where(s < 7, 1, 0)
    for k in RELAYS[0] + RELAYS[1]:
        extra = extra + jnp.where(xy == k, 1, 0)

    def send_partial(q, peer):
        pltpu.make_async_remote_copy(
            src_ref=part.at[q], dst_ref=recv_a.at[q_me], send_sem=sa, recv_sem=ra,
            device_id=peer, device_id_type=MESH,
        ).start()

    for g in range(4):
        q0 = g * 8
        loads[2 + g].wait()
        acc = dot(rad[q0 : q0 + 8, 0].reshape(128, 2048), d0[...], NT)
        acc = acc + dot(rad[q0 : q0 + 8, 1].reshape(128, 2048), d1[...], NT)
        part[q0 : q0 + 8] = acc.reshape(8, 16, 128).astype(BF)
        if g == 2:
            load_rest()
        if g == GREETED:
            pl.semaphore_wait(barrier, 40 + extra)
        for t in range(g + 1) if g == GREETED else [g] if g > GREETED else []:
            px = [(t % 2) * 2 + lax.rem(cx + dx, 2) for dx in range(2)]
            for dx in (1, 0):
                for dy in (2, 1, 3, 0):
                    q = px[dx] * 4 + ys[dy]
                    peer = (own_z + t // 2, own_half + q)
                    q = q + (t // 2) * 16
                    if dy != 0:
                        send_partial(q, peer)
                    else:

                        @pl.when(q != q_me)
                        def _():
                            send_partial(q, peer)

    @pl.when(s < 7)
    def _():
        for v in range(5):
            pltpu.make_async_remote_copy(
                src_ref=state_hbm.at[pl.ds(v * 64 + 48, 16), pl.ds(24, 8)],
                dst_ref=ax_recv.at[0, pl.ds(v * 16, 16)],
                send_sem=hx_s.at[0], recv_sem=hx_r.at[0],
                device_id=(s + 1, a), device_id_type=MESH).start()

    @pl.when(s > 0)
    def _():
        for v in range(5):
            pltpu.make_async_remote_copy(
                src_ref=state_hbm.at[pl.ds(v * 64, 16), pl.ds(0, 8)],
                dst_ref=ax_recv.at[1, pl.ds(v * 16, 16)],
                send_sem=hx_s.at[1], recv_sem=hx_r.at[1],
                device_id=(s - 1, a), device_id_type=MESH).start()

    recv_a[q_me] = part[q_me]

    loads[6].wait()

    @pl.loop(0, 40)
    def _(i):
        for j in range(8):
            c = i * 8 + j
            sf[pl.ds(c * PITCH, ROWS), :] = st[c].astype(F32)

    @pl.loop(0, 4)
    def _(x):
        for rhi in range(2):
            col = pl.multiple_of(x * 256 + rhi * 128, 128)
            last = sf[pl.ds(x * 8 + rhi * 4 + 3, 320, stride=PITCH), :].reshape(10, 2, 2, 8, 128)
            packed = jnp.concatenate([last[:, 0, 1, 4:8], last[:, 1, 1, 4:8]], axis=1)
            az_send[0, :, pl.ds(col, 128)] = packed.reshape(80, 128).astype(BF)
            head = sf[pl.ds(x * 8 + rhi * 4, 320, stride=PITCH), :].reshape(10, 2, 2, 8, 128)
            packed = jnp.concatenate([head[:, 0, 0, 0:4], head[:, 1, 0, 0:4]], axis=1)
            az_send[1, :, pl.ds(col, 128)] = packed.reshape(80, 128).astype(BF)

    def az_copy(way, dst):
        return pltpu.make_async_remote_copy(
            src_ref=az_send.at[way], dst_ref=az_recv.at[way], send_sem=ha_s.at[way],
            recv_sem=ha_r.at[way], device_id=(s, dst), device_id_type=MESH)

    az_up, az_dn = az_copy(0, a_next), az_copy(1, a_prev)
    for way, dst in ((0, a_next), (1, a_prev)):

        @pl.when(xy == ends[way])
        def _():
            for i, k in enumerate(RELAYS[way]):
                pltpu.make_async_remote_copy(
                    src_ref=az_send.at[way, pl.ds(16 * i + 16, 16)], dst_ref=relay,
                    send_sem=ha_s.at[way], recv_sem=rel_r,
                    device_id=(s, z_hi * 16 + k), device_id_type=MESH).start()
            piece = pl.ds(0, 16)
            pltpu.make_async_remote_copy(
                src_ref=az_send.at[way, piece], dst_ref=az_recv.at[way, piece],
                send_sem=ha_s.at[way], recv_sem=ha_r.at[way],
                device_id=(s, dst), device_id_type=MESH).start()

    lane = lax.broadcasted_iota(jnp.int32, (80, 128), 1)

    @pl.loop(0, 4)
    def _(x):
        for ay in range(4):
            roll_up, roll_dn = [], []
            for rhi in range(2):
                r = x * 8 + rhi * 4 + ay
                col = pl.multiple_of(x * 256 + rhi * 128, 128)
                f = sf[pl.ds(r, 320, stride=PITCH), :]
                xb = f.astype(BF)
                rhs[ay, 640:960, pl.ds(col, 128)] = xb
                x5 = xb.reshape(5, 64, 128)

                @pl.when(x < 3)
                def _():
                    rhs[ay, 0:80, pl.ds(col + 256, 128)] = x5[:, 48:64].reshape(80, 128)

                @pl.when(x > 0)
                def _():
                    rhs[ay, 80:160, pl.ds(col - 256, 128)] = x5[:, 0:16].reshape(80, 128)

                tiles = f.reshape(20, 2, 8, 128)
                upper = tiles[:, 1]
                lower = tiles[:, 0]
                if ay < 3:
                    rhs[ay + 1, 160:320, pl.ds(col, 128)] = upper.reshape(160, 128).astype(BF)
                if ay > 0:
                    rhs[ay - 1, 320:480, pl.ds(col, 128)] = lower.reshape(160, 128).astype(BF)
                roll_up.append(pltpu.roll(sf[pl.ds(3 * PITCH + r, 80, stride=4 * PITCH), :], 1, 1))
                roll_dn.append(pltpu.roll(sf[pl.ds(r, 80, stride=4 * PITCH), :], 127, 1))
            col = pl.multiple_of(x * 256, 256)
            zero = jnp.zeros((80, 128), F32)
            rhs[ay, 480:560, pl.ds(col, 128)] = jnp.where(lane == 0, zero, roll_up[0]).astype(BF)
            rhs[ay, 480:560, pl.ds(col + 128, 128)] = jnp.where(lane == 0, roll_up[0], roll_up[1]).astype(BF)
            rhs[ay, 560:640, pl.ds(col, 128)] = jnp.where(lane == 127, roll_dn[1], roll_dn[0]).astype(BF)
            rhs[ay, 560:640, pl.ds(col + 128, 128)] = jnp.where(lane == 127, zero, roll_dn[1]).astype(BF)

    @pl.when(xy < 15)
    def _():
        az_up.start()

    @pl.when(xy > 0)
    def _():
        az_dn.start()

    @pl.when(s == 0)
    def _():
        rhs[:, 0:80, 0:256] = jnp.zeros((4, 80, 256), BF)

    @pl.when(s == 7)
    def _():
        rhs[:, 80:160, 768:1024] = jnp.zeros((4, 80, 256), BF)

    for i in (10, 11, 12, 13, 14, 15):
        loads[i].wait()
    for c0, c1 in ((0, 128), (128, 256), (256, 320)):
        line = prof_ref[c0:c1].reshape(1, c1 - c0)
        prof_rows[c0:c1, :] = jnp.transpose(jnp.broadcast_to(line, (128, c1 - c0)))
    kb = pl.multiple_of((q_me // 4) * 128, 128)
    row = pl.multiple_of((q_me % 4) * 32, 32)

    def packed_columns(block):
        tcol[...] = jnp.transpose(block)
        return jnp.concatenate(
            [tcol[pl.ds(row, 16), :], tcol[pl.ds(pl.multiple_of(row + 16, 16), 16), :]], axis=1)

    target_own = packed_columns(target[:, pl.ds(kb, 128)])
    weight_own = packed_columns(taper_ref[...] * wobs_ref[:, pl.ds(kb, 128)])

    pltpu.make_async_copy(part.at[pl.ds(0, 31)], recv_a.at[pl.ds(0, 31)], ra).wait()
    send_b[...] = jnp.sum(recv_a[...].astype(F32), axis=0).astype(BF)
    for dz in (4, 3, 5, 2, 6, 1, 7):
        pltpu.make_async_remote_copy(
            src_ref=send_b, dst_ref=recv_b.at[z_me], send_sem=sb, recv_sem=rb,
            device_id=z_peer(dz), device_id_type=MESH,
        ).start()
    recv_b[z_me] = send_b[...]

    def forward(way):
        for i, k in enumerate(RELAYS[way]):

            @pl.when(xy == k)
            def _():
                pltpu.make_async_copy(az_send.at[0, pl.ds(0, 16)], relay, rel_r).wait()
                rows = pl.ds(16 * i + 16, 16)
                pltpu.make_async_remote_copy(
                    src_ref=relay, dst_ref=az_recv.at[way, rows], send_sem=rel_s, recv_sem=ha_r.at[way],
                    device_id=(s, (1 - z_hi) * 16 + ends[1 - way]), device_id_type=MESH).start()

    forward(0)
    forward(1)

    for i in (7, 8, 9):
        loads[i].wait()
    lf[:, 0:640] = dot(lift[...], exp[...]).astype(BF)
    lf[:, 640:960] = vol[...]

    def sector_row(ay):
        res = dot(lf[...], rhs[ay])
        for x in range(4):
            for rhi in range(2):
                at = (pl.ds(x * 8 + rhi * 4 + ay, 320, stride=PITCH), slice(None))
                col = x * 256 + rhi * 128
                sf[at] = sf[at] + res[:, col : col + 128]

    def axial_halo(side, row, col):
        pltpu.make_async_copy(az_send.at[0], az_recv.at[0], hx_r.at[side]).wait()
        for c in range(80):
            axf[c * FACE_PITCH : c * FACE_PITCH + 8, :] = ax_recv[side, c].astype(F32)
        for rhi in range(2):
            for ay in range(4):
                face = axf[pl.ds(rhi * 4 + ay, 80, stride=FACE_PITCH), :].astype(BF)
                rhs[ay, row : row + 80, col + rhi * 128 : col + rhi * 128 + 128] = face

    @pl.when(s > 0)
    def _():
        axial_halo(0, 0, 0)

    @pl.when(s < 7)
    def _():
        axial_halo(1, 80, 768)

    @pl.loop(1, 3)
    def _(ay):
        sector_row(ay)

    pltpu.make_async_copy(part.at[pl.ds(0, 7)], recv_b.at[pl.ds(0, 7)], rb).wait()
    total = jnp.sum(recv_b[...].astype(F32), axis=0)
    own = weight_own * (total - target_own)
    own_f[...] = own
    sens[q_me] = own.astype(BF)
    for step in sorted(steps, key=lambda t: t[2]):
        pltpu.make_async_remote_copy(
            src_ref=sens.at[q_me], dst_ref=sens.at[q_me], send_sem=sc,
            recv_sem=rc.at[step[2]],
            device_id=group_peer(step), device_id_type=MESH,
        ).start()
    swap = pltpu.make_async_remote_copy(
        src_ref=own_f, dst_ref=other_f, send_sem=sp, recv_sem=rp,
        device_id=((s + 1) - 2 * core, a), device_id_type=MESH)
    swap.start()

    w_hi, w_lo = halves(wsam_ref[...])
    w_lo2 = (wsam_ref[...] - w_hi.astype(F32) - w_lo.astype(F32)).astype(BF)
    w3 = jnp.concatenate([w_hi, w_lo, w_lo2], axis=0)
    g_rows = [jnp.sum(dot(w3, ret[b]), axis=0, keepdims=True) for b in range(16)]
    g_hi, g_lo = halves(jnp.concatenate(g_rows, axis=0))
    gg = jnp.concatenate([g_hi, g_lo], axis=0)
    blank = jnp.zeros((32, 64), BF)
    g0[...] = jnp.concatenate([gg, blank], axis=1)
    g1[...] = jnp.concatenate([blank, gg], axis=1)
    host = host_ref[...]
    lo = host % 128
    oh_lo[...] = jnp.where(lax.broadcasted_iota(jnp.int32, (128, 2048), 0) == lo, 1.0, 0.0).astype(BF)
    hi = host // 128
    point_row = (hi // 8) * 8 + (hi % 2) * 4 + (hi // 2) % 4

    az_up.wait()
    az_dn.wait()
    for x in range(4):
        for rhi in range(2):
            src = slice(x * 256 + rhi * 128, x * 256 + rhi * 128 + 128)
            up = az_recv[0, :, src].astype(F32).reshape(10, 8, 128)
            even = jnp.concatenate([up[:, 4:8], up[:, 0:4]], axis=1)
            both = jnp.concatenate([even[:, None], up[:, None]], axis=1)
            rhs[0, 160:320, src] = both.reshape(160, 128).astype(BF)
            dn = az_recv[1, :, src].astype(F32).reshape(10, 8, 128)
            odd = jnp.concatenate([dn[:, 4:8], dn[:, 0:4]], axis=1)
            both = jnp.concatenate([dn[:, None], odd[:, None]], axis=1)
            rhs[3, 320:480, src] = both.reshape(160, 128).astype(BF)

    @pl.loop(0, 2)
    def _(i):
        sector_row(i * 3)

    def strengths(group):
        chunks = pl.ds(cs[group] * 16, 16)
        flat = sens[chunks].reshape(256, 128)
        low = []
        for g in (g0, g1):
            h = dot(g[...], flat, NT)
            low.append(jnp.concatenate(halves(h[0:16] + h[16:32]), axis=0))
        for n in range(4):
            cols = slice(n * 512, n * 512 + 512)
            val = 0.0
            for half in range(2):
                val = val + dot(low[half], rad[chunks, half, :, cols].reshape(256, 512))
            yield cols, val

    pltpu.make_async_copy(sens.at[pl.ds(0, 15)], sens.at[pl.ds(0, 15)], rc.at[0]).wait()
    for cols, val in strengths(0):
        first[:, cols] = val
    pltpu.make_async_copy(sens.at[pl.ds(0, 16)], sens.at[pl.ds(0, 16)], rc.at[1]).wait()
    block_of = lax.broadcasted_iota(jnp.int32, (32, 512), 0) % 16
    rows = lax.broadcasted_iota(jnp.int32, (32, 512), 0)
    es = jnp.zeros((64, 128), F32)
    for n, (cols, val) in enumerate(strengths(1)):
        mine = lax.broadcasted_iota(jnp.int32, (32, 512), 1) // 128 + n * 4 == block_of
        strength = jnp.sum(jnp.where(mine, first[:, cols] + val, 0.0), axis=0, keepdims=True)
        spread_rows = jnp.where(rows == point_row[:, cols], strength, 0.0)
        pieces = jnp.concatenate(halves(spread_rows), axis=0)
        es = es + dot(pieces, oh_lo[:, cols], NT)
    es_ref[...] = es[0:32] + es[32:64]

    swap.wait()
    mine_f = jnp.where(core == z_hi, own_f[...], other_f[...])
    obs_ref[0:16, :] = mine_f[:, 0:64]
    obs_ref[16:32, :] = mine_f[:, 64:128]

    pltpu.make_async_copy(part.at[pl.ds(0, 31)], recv_a.at[pl.ds(0, 31)], sa).wait()
    pltpu.make_async_copy(part.at[pl.ds(0, 7)], recv_b.at[pl.ds(0, 7)], sb).wait()
    pltpu.make_async_copy(sens.at[pl.ds(0, 31)], sens.at[pl.ds(0, 31)], sc).wait()

    @pl.when(s < 7)
    def _():
        pltpu.make_async_copy(az_send.at[0], az_recv.at[0], hx_s.at[0]).wait()

    @pl.when(s > 0)
    def _():
        pltpu.make_async_copy(az_send.at[0], az_recv.at[0], hx_s.at[1]).wait()

    for k in RELAYS[0] + RELAYS[1]:

        @pl.when(xy == k)
        def _():
            pltpu.make_async_copy(az_send.at[0, pl.ds(0, 16)], relay, rel_s).wait()


def finish(base_ref, es_ref, prof_ref, obs_in, out_hbm, obs_out, buf, sems):
    copies = [pltpu.make_async_copy(obs_in, obs_out, sems.at[FINISH])]
    copies[0].start()
    es = es_ref[...]
    for k in range(FINISH):
        n = 320 // FINISH

        @pl.loop(0, n // 8)
        def _(i):
            for j in range(8):
                c = k * n + i * 8 + j
                rows = pl.ds(pl.multiple_of(c * ROWS, ROWS), ROWS)
                buf[rows, :] = base_ref[pl.ds(c * PITCH, ROWS), :] + prof_ref[pl.ds(c, 1), :] * es

        part = pl.ds(k * n * ROWS, n * ROWS)
        copies.append(pltpu.make_async_copy(buf.at[part], out_hbm.at[part], sems.at[k]))
        copies[-1].start()
    for c in copies:
        c.wait()


def hann_taper(count):
    samples = np.arange(count, dtype=np.float32)
    return (0.5 - 0.5 * np.cos(2.0 * np.pi * (samples + 0.5) / count)).astype(np.float32)


def body(
    surface_signal, retarded_weights, radiation_weights, target_signal, observer_weights,
    sample_weights, host_element, source_profile, adjoint_state, volume_operator, lift_operator,
):
    dma = pltpu.SemaphoreType.DMA
    state = adjoint_state.reshape(320, 4, 4, 2, 128).transpose(0, 1, 3, 2, 4).reshape(320, 32, 128)
    taper = jnp.asarray(np.repeat(hann_taper(64)[:, None], 128, axis=1))
    expand = jnp.asarray(expander(), dtype=BF)
    base, obs_t, es, prof_rows = pl.pallas_call(
        kernel,
        out_shape=(
            pltpu.VMEM((320 * PITCH, 128), F32),
            jax.ShapeDtypeStruct((32, 64), F32),
            jax.ShapeDtypeStruct((32, 128), F32),
            pltpu.VMEM((320, 128), F32),
        ),
        in_specs=[ANY] * 13,
        out_specs=(VM, VM, VM, VM),
        scratch_shapes=[
            pltpu.VMEM((64, 2048), BF),
            pltpu.VMEM((16, 64, 64), BF),
            pltpu.VMEM((32, 2, 16, 2048), BF),
            pltpu.VMEM((320, 32, 128), BF),
            pltpu.VMEM((320, 480), BF),
            pltpu.VMEM((320, 320), BF),
            pltpu.VMEM((480, 640), BF),
            pltpu.VMEM((64, 1024), F32),
            pltpu.VMEM((128, 2048), BF),
            pltpu.VMEM((128, 2048), BF),
            pltpu.VMEM((32, 128), BF),
            pltpu.VMEM((32, 128), BF),
            pltpu.VMEM((32, 16, 128), BF),
            pltpu.VMEM((32, 16, 128), BF),
            pltpu.VMEM((16, 128), BF),
            pltpu.VMEM((8, 16, 128), BF),
            pltpu.VMEM((32, 16, 128), BF),
            pltpu.VMEM((16, 128), F32),
            pltpu.VMEM((16, 128), F32),
            pltpu.VMEM((4, 960, 1024), BF),
            pltpu.VMEM((320, 960), BF),
            pltpu.VMEM((2, 80, 1024), BF),
            pltpu.VMEM((2, 80, 1024), BF),
            pltpu.VMEM((2, 80, 8, 128), BF),
            pltpu.VMEM((80 * FACE_PITCH, 128), F32),
            pltpu.VMEM((128, 2048), BF),
            pltpu.VMEM((128, 64), F32),
            pltpu.VMEM((64, 128), F32),
            pltpu.VMEM((1, 1024), F32),
            pltpu.VMEM((1, 64), F32),
            pltpu.VMEM((1, 2048), jnp.int32),
            pltpu.VMEM((320,), F32),
            pltpu.VMEM((16, 1024), BF),
            pltpu.VMEM((32, 2048), F32),
            dma((16,)),
            dma, dma, dma, dma, dma, dma((2,)), dma, dma,
            dma((2,)), dma((2,)), dma((2,)), dma((2,)), dma, dma,
        ],
        compiler_params=pltpu.CompilerParams(
            collective_id=0, has_side_effects=True, vmem_limit_bytes=48 * 1024 * 1024
        ),
    )(
        *(
            pltpu.with_memory_space_constraint(x, pltpu.HBM)
            for x in (
                surface_signal,
                retarded_weights,
                radiation_weights.reshape(32, 2, 16, 2048),
                state,
                lift_operator,
                volume_operator,
                expand,
                target_signal,
                taper,
                observer_weights.reshape(1, 1024),
                sample_weights.reshape(1, 64),
                host_element.reshape(1, 2048),
                source_profile,
            )
        )
    )
    updated, obs_t = pl.pallas_call(
        finish,
        out_shape=(
            jax.ShapeDtypeStruct((10240, 128), F32),
            jax.ShapeDtypeStruct((32, 64), F32),
        ),
        in_specs=[VM, VM, VM, VM],
        out_specs=(ANY, ANY),
        scratch_shapes=[pltpu.VMEM((10240, 128), F32), dma((FINISH + 1,))],
        compiler_params=pltpu.CompilerParams(vmem_limit_bytes=16 * 1024 * 1024),
    )(
        pltpu.with_memory_space_constraint(base, pltpu.VMEM),
        es,
        pltpu.with_memory_space_constraint(prof_rows, pltpu.VMEM),
        obs_t,
    )
    updated = updated.reshape(320, 4, 2, 4, 128).transpose(0, 1, 3, 2, 4)
    return (obs_t.T, updated.reshape(320, 4, 4, 256))


def solution(mesh):
    return jax.shard_map(
        body,
        mesh=mesh,
        in_specs=(
            P(None, ("stream", "azim")),
            P(("stream", "azim"), None, None),
            P(None, ("stream", "azim")),
            P(),
            P(),
            P(),
            P(("stream", "azim")),
            P(),
            P(None, "stream", "azim", None),
            P(),
            P(),
        ),
        out_specs=(P(None, "azim"), P(None, "stream", "azim", None)),
        check_vma=False,
    )
```
